128 devices in a mesh: gx: 8 (over x, z_lo), gy: 16 (over y, z_hi, core).
Axes of the slice: x: 4, y: 4, z: 4 (z_hi: 2, z_lo: 2; z = z_hi * 2 + z_lo), core: 2. Of those that a mesh axis runs over, the one named last changes fastest.
Arguments:
- images: bfloat16 [64, 2, 1024, 1024], P('gy', None, 'gx'), may hold values from -192 to 192
- rates: float32 [256], replicated, may hold values from 0.002 to 0.2
- smoothing: float32 [256], replicated, may hold values from 0.02 to 1
Outputs:
- spectra: float32 [2, 1024, 1024, 256], P(None, 'gx', 'gy')
The draws below stay inside these ranges and needn't reach their ends.
All inputs are finite; a program needn't handle non-finite values.
Results may differ from the reference program's by a relative error of at most 0.0033.
Values may be sent and summed in bfloat16 or wider, within the bound.
A program may use at most 192 MiB of HBM per device.

```python
import math
import jax
import jax.numpy as jnp
from jax import lax

E = 64
R = 256
SL = 2
ITERS = 3
H = 1024
W = 1024


def draw_rates(key, part):
    spread_count = max(2, R // 32)
    low_log = math.log(0.002)
    mid_log = math.log(0.1)
    high_log = math.log(0.2)
    width = (mid_log - low_log) / spread_count
    first_key = jax.random.fold_in(key, 11)
    second_key = jax.random.fold_in(key, 23)
    third_key = jax.random.fold_in(key, 37)
    offsets = jax.random.uniform(first_key, (spread_count,), dtype=jnp.float32)
    spread_logs = low_log + width * (jnp.arange(spread_count, dtype=jnp.float32) + offsets)
    dense_logs = jax.random.uniform(second_key, (R - spread_count,), dtype=jnp.float32, minval=mid_log, maxval=high_log)
    all_logs = jnp.concatenate([spread_logs, dense_logs])
    order = jax.random.permutation(third_key, R)
    return jnp.exp(all_logs[order]).astype(jnp.float32)


def shard_levels(own_key, shape, cuts, low, high):
    loudness = 1.0
    for axis_at, shards_of in cuts:
        steps = jax.random.uniform(jax.random.fold_in(jax.random.fold_in(own_key, 6), axis_at), (shards_of,), jnp.float32, low / len(cuts), high / len(cuts))
        loudness = loudness * jnp.repeat(jnp.exp(steps), shape[axis_at] // shards_of).reshape((-1,) + (1,) * (len(shape) - 1 - axis_at))
    return loudness


def scatter_about(key, shape, scale, reach, split=(), kind=jnp.bfloat16):
    values = scale * jax.random.normal(key, shape, jnp.float32)
    if split:
        values = values * shard_levels(key, shape, split, -0.22, 0.18)
    return jnp.clip(values, -reach, reach).astype(kind)


def setup_inputs(seed: int = 0) -> dict:
    streams_of = jax.random.split(jax.random.key(seed), 4)
    return {
        "images": scatter_about(streams_of[0], (E, SL, H, W), 32.0, 192.0, ((0, 16), (2, 8))),
        "rates": draw_rates(jax.random.fold_in(streams_of[3], 71), 0),
        "smoothing": jnp.clip(jnp.exp(jax.random.uniform(streams_of[2], (R,), jnp.float32, math.log(0.02), math.log(1.0))), 0.02, 1.0),
    }


def kernel_parts(rates, smoothing):
    times = 10.0 * (jnp.arange(E, dtype=jnp.float32) + 1.0)
    raw = jnp.exp(-times[:, None] * rates[None, :])
    kernel = raw / jnp.sqrt(lax.optimization_barrier(jnp.sum(raw * raw, axis=0)))[None, :]
    gram = jnp.dot(kernel.T, kernel, precision=lax.Precision.HIGHEST)
    rowsum = lax.optimization_barrier(jnp.sum(gram, axis=1))
    lam = smoothing * rowsum
    step = 1.0 / (rowsum + 8.0 * lam)
    return (kernel, gram, lam, step)

def laplace(field):
    padded = jnp.pad(field, ((1, 1), (1, 1), (0, 0)))
    center = padded[1:-1, 1:-1]
    return 4.0 * center - padded[2:, 1:-1] - padded[:-2, 1:-1] - padded[1:-1, 2:] - padded[1:-1, :-2]

def reference(images, rates, smoothing):
    kernel, gram, lam, step = kernel_parts(rates, smoothing)
    kernel_b = kernel.astype(jnp.bfloat16).astype(jnp.float32)

    def one_slice(slab):
        rows, cols = (slab.shape[1], slab.shape[2])
        proj = jnp.einsum('eij,er->ijr', slab.astype(jnp.float32), kernel_b, precision=lax.Precision.HIGHEST)
        field = jnp.maximum(proj * step, 0.0)
        for count in range(ITERS - 1):
            curved = jnp.dot(field.reshape(rows * cols, R), gram, precision=lax.Precision.HIGHEST).reshape(rows, cols, R)
            grad = curved - proj + lam * laplace(field)
            field = jnp.maximum(field - step * grad, 0.0)
        return field
    return lax.map(one_slice, jnp.transpose(images, (1, 0, 2, 3)))
```

```python
import functools

import jax
import jax.numpy as jnp
from jax import lax
from jax.experimental import pallas as pl
from jax.experimental.pallas import tpu as pltpu
from jax.sharding import PartitionSpec as P

E = 64
ITERS = 3
RH = 2
CH = 4
TR = 16


def kernel_parts(rates, smoothing):
    times = 10.0 * (jnp.arange(E, dtype=jnp.float32) + 1.0)
    raw = jnp.exp(-times[:, None] * rates[None, :])
    kernel = raw / jnp.sqrt(jnp.sum(raw * raw, axis=0))[None, :]
    gram = jnp.dot(kernel.T, kernel, precision=lax.Precision.HIGHEST)
    rowsum = jnp.sum(gram, axis=1)
    lam = smoothing * rowsum
    step = 1.0 / (rowsum + 8.0 * lam)
    return (kernel, gram, lam, step)


def halo(cells, axis, dim, width):
    count = lax.axis_size(axis)
    head = lax.slice_in_dim(cells, 0, width, axis=dim)
    tail = lax.slice_in_dim(cells, cells.shape[dim] - width, cells.shape[dim], axis=dim)
    return jnp.concatenate(
        [
            lax.ppermute(tail, axis, [(i, i + 1) for i in range(count - 1)]),
            cells,
            lax.ppermute(head, axis, [(i + 1, i) for i in range(count - 1)]),
        ],
        axis=dim,
    )


def split3(f):
    hi = f.astype(jnp.bfloat16)
    lo = (f - hi.astype(jnp.float32)).astype(jnp.bfloat16)
    return jnp.concatenate([hi, lo, hi], axis=1)


def fit_kernel(wp, x_ref, kb_ref, g3_ref, step_ref, lam_ref, cm_ref, rm_ref,
               o_ref, b_ref, f0_ref, f1_ref, f3_ref, m_ref):
    t = pl.program_id(1)
    rows = TR + 2 * RH
    n = rows * wp
    base = pl.multiple_of(t * (TR * wp), 16)
    step = step_ref[...]
    lam = lam_ref[...]
    cm = cm_ref[...]

    b = jnp.dot(x_ref[0, pl.ds(base, n), :], kb_ref[...],
                preferred_element_type=jnp.float32)
    b_ref[...] = b
    f0 = jnp.maximum(b * step, 0.0)
    f0_ref[...] = f0
    f3_ref[...] = split3(f0)

    def update(src_ref, q):
        o = pl.multiple_of(q * wp, 8)
        c = src_ref[pl.ds(o, wp), :]
        up = src_ref[pl.ds(o - wp, wp), :]
        dn = src_ref[pl.ds(o + wp, wp), :]
        lf = pltpu.roll(c, 1, 0)
        rt = pltpu.roll(c, wp - 1, 0)
        lap = 4.0 * c - up - dn - lf - rt
        m = m_ref[pl.ds(o - wp, wp), :]
        g = m - b_ref[pl.ds(o, wp), :] + lam * lap
        return jnp.maximum(c - step * g, 0.0)

    m_ref[...] = jnp.dot(f3_ref[pl.ds(wp, (rows - 2) * wp), :], g3_ref[...],
                         preferred_element_type=jnp.float32)

    def body1(q, carry):
        f1 = update(f0_ref, q) * (cm * rm_ref[t * TR + q])
        f1_ref[pl.ds(pl.multiple_of(q * wp, 8), wp), :] = f1
        return carry

    lax.fori_loop(1, rows - 1, body1, 0)
    f1_ref[pl.ds(0, wp), :] = jnp.zeros((wp, f1_ref.shape[1]), jnp.float32)
    f1_ref[pl.ds((rows - 1) * wp, wp), :] = jnp.zeros((wp, f1_ref.shape[1]), jnp.float32)

    f3_ref[...] = split3(f1_ref[...])
    m_ref[...] = jnp.dot(f3_ref[pl.ds(wp, (rows - 2) * wp), :], g3_ref[...],
                         preferred_element_type=jnp.float32)

    def body2(q, carry):
        f2 = update(f1_ref, q)
        f2 = pltpu.roll(f2, wp - CH, 0)
        o_ref[0, q - RH] = f2[: wp - 2 * CH]
        return carry

    lax.fori_loop(RH, rows - RH, body2, 0)


def per_device(images, rates, smoothing):
    kernel, gram, lam, step = kernel_parts(rates, smoothing)
    kb = kernel.astype(jnp.bfloat16)
    gh = gram.astype(jnp.bfloat16)
    gl = (gram - gh.astype(jnp.float32)).astype(jnp.bfloat16)
    g3 = jnp.concatenate([gh, gh, gl], axis=0)
    x = lax.all_to_all(images, "gy", split_axis=3, concat_axis=0, tiled=True)
    e, sl, h, w = x.shape
    x = halo(x, "gy", 3, CH)
    x = halo(x, "gx", 2, RH)
    hp, wp = h + 2 * RH, w + 2 * CH
    x = jnp.transpose(x, (1, 2, 3, 0)).reshape(sl, hp * wp, e)
    r = kernel.shape[1]

    gi = lax.axis_index("gx")
    gj = lax.axis_index("gy")
    grow = gi * h + jnp.arange(hp) - RH
    rm = ((grow >= 0) & (grow < h * lax.axis_size("gx"))).astype(jnp.float32)
    gcol = gj * w + jnp.arange(wp) - CH
    cv = ((gcol >= 0) & (gcol < w * lax.axis_size("gy"))).astype(jnp.float32)
    cm = jnp.broadcast_to(cv[:, None], (wp, r))

    rows = TR + 2 * RH
    nt = h // TR
    flops = 2 * sl * nt * rows * wp * r * (e + 2 * 3 * r)
    out = pl.pallas_call(
        functools.partial(fit_kernel, wp),
        out_shape=jax.ShapeDtypeStruct((sl, h, w, r), jnp.float32),
        grid=(sl, nt),
        in_specs=[
            pl.BlockSpec((1, hp * wp, e), lambda s, t: (s, 0, 0)),
            pl.BlockSpec((e, r), lambda s, t: (0, 0)),
            pl.BlockSpec((3 * r, r), lambda s, t: (0, 0)),
            pl.BlockSpec((1, r), lambda s, t: (0, 0)),
            pl.BlockSpec((1, r), lambda s, t: (0, 0)),
            pl.BlockSpec((wp, r), lambda s, t: (0, 0)),
            pl.BlockSpec(memory_space=pltpu.SMEM),
        ],
        out_specs=pl.BlockSpec((1, TR, w, r), lambda s, t: (s, t, 0, 0)),
        scratch_shapes=[
            pltpu.VMEM((rows * wp, r), jnp.float32),
            pltpu.VMEM((rows * wp, r), jnp.float32),
            pltpu.VMEM((rows * wp, r), jnp.float32),
            pltpu.VMEM((rows * wp, 3 * r), jnp.bfloat16),
            pltpu.VMEM(((rows - 2) * wp, r), jnp.float32),
        ],
        compiler_params=pltpu.CompilerParams(
            dimension_semantics=("arbitrary", "arbitrary"),
            vmem_limit_bytes=48 * 1024 * 1024,
        ),
        cost_estimate=pl.CostEstimate(
            flops=flops, transcendentals=0,
            bytes_accessed=sl * (hp * wp * e * 2 + h * w * r * 4),
        ),
    )(x, kb, g3, step[None, :], lam[None, :], cm, rm)
    return out


def solution(mesh):
    in_specs = (P("gy", None, "gx", None), P(), P())
    out_specs = P(None, "gx", "gy", None)
    return jax.shard_map(
        per_device, mesh=mesh, in_specs=in_specs, out_specs=out_specs, check_vma=False
    )
```

```python
import functools

import jax
import jax.numpy as jnp
from jax import lax
from jax.experimental import pallas as pl
from jax.experimental.pallas import tpu as pltpu
from jax.sharding import PartitionSpec as P

E = 64
ITERS = 3
RH = 2
CH = 4
TR = 16


def kernel_parts(rates, smoothing):
    times = 10.0 * (jnp.arange(E, dtype=jnp.float32) + 1.0)
    raw = jnp.exp(-times[:, None] * rates[None, :])
    kernel = raw / jnp.sqrt(jnp.sum(raw * raw, axis=0))[None, :]
    gram = jnp.dot(kernel.T, kernel, precision=lax.Precision.HIGHEST)
    rowsum = jnp.sum(gram, axis=1)
    lam = smoothing * rowsum
    step = 1.0 / (rowsum + 8.0 * lam)
    return (kernel, gram, lam, step)


def halo(cells, axis, dim, width):
    count = lax.axis_size(axis)
    head = lax.slice_in_dim(cells, 0, width, axis=dim)
    tail = lax.slice_in_dim(cells, cells.shape[dim] - width, cells.shape[dim], axis=dim)
    return jnp.concatenate(
        [
            lax.ppermute(tail, axis, [(i, i + 1) for i in range(count - 1)]),
            cells,
            lax.ppermute(head, axis, [(i + 1, i) for i in range(count - 1)]),
        ],
        axis=dim,
    )


def split3(f):
    hi = f.astype(jnp.bfloat16)
    lo = (f - hi.astype(jnp.float32)).astype(jnp.bfloat16)
    return jnp.concatenate([hi, lo, hi], axis=1)


def fit_kernel(wp, x_ref, kb_ref, g3_ref, step_ref, lam_ref, cm_ref, rm_ref,
               o_ref, b_ref, f0_ref, f1_ref, f3_ref, m_ref):
    t = pl.program_id(1)
    rows = TR + 2 * RH
    n = rows * wp
    base = pl.multiple_of(t * (TR * wp), 16)
    step = step_ref[...]
    lam = lam_ref[...]
    cm = cm_ref[...]

    kb = kb_ref[...]

    def body0(q, carry):
        xp = x_ref[0, t * TR + q]
        bq = lax.dot_general(xp, kb, (((0,), (0,)), ((), ())),
                             preferred_element_type=jnp.float32)
        o = pl.multiple_of(q * wp, 8)
        b_ref[pl.ds(o, wp), :] = bq
        f0_ref[pl.ds(o, wp), :] = jnp.maximum(bq * step, 0.0)
        return carry

    lax.fori_loop(0, rows, body0, 0)
    f3_ref[...] = split3(f0_ref[...])

    def update(src_ref, q):
        o = pl.multiple_of(q * wp, 8)
        c = src_ref[pl.ds(o, wp), :]
        up = src_ref[pl.ds(o - wp, wp), :]
        dn = src_ref[pl.ds(o + wp, wp), :]
        lf = pltpu.roll(c, 1, 0)
        rt = pltpu.roll(c, wp - 1, 0)
        lap = 4.0 * c - up - dn - lf - rt
        m = m_ref[pl.ds(o - wp, wp), :]
        g = m - b_ref[pl.ds(o, wp), :] + lam * lap
        return jnp.maximum(c - step * g, 0.0)

    m_ref[...] = jnp.dot(f3_ref[pl.ds(wp, (rows - 2) * wp), :], g3_ref[...],
                         preferred_element_type=jnp.float32)

    def body1(q, carry):
        f1 = update(f0_ref, q) * (cm * rm_ref[t * TR + q])
        f1_ref[pl.ds(pl.multiple_of(q * wp, 8), wp), :] = f1
        return carry

    lax.fori_loop(1, rows - 1, body1, 0)
    f1_ref[pl.ds(0, wp), :] = jnp.zeros((wp, f1_ref.shape[1]), jnp.float32)
    f1_ref[pl.ds((rows - 1) * wp, wp), :] = jnp.zeros((wp, f1_ref.shape[1]), jnp.float32)

    f3_ref[...] = split3(f1_ref[...])
    m_ref[...] = jnp.dot(f3_ref[pl.ds(wp, (rows - 2) * wp), :], g3_ref[...],
                         preferred_element_type=jnp.float32)

    def body2(q, carry):
        f2 = update(f1_ref, q)
        f2 = pltpu.roll(f2, wp - CH, 0)
        o_ref[0, q - RH] = f2[: wp - 2 * CH]
        return carry

    lax.fori_loop(RH, rows - RH, body2, 0)


def per_device(images, rates, smoothing):
    kernel, gram, lam, step = kernel_parts(rates, smoothing)
    kb = kernel.astype(jnp.bfloat16)
    gh = gram.astype(jnp.bfloat16)
    gl = (gram - gh.astype(jnp.float32)).astype(jnp.bfloat16)
    g3 = jnp.concatenate([gh, gh, gl], axis=0)
    x = lax.all_to_all(images, "gy", split_axis=3, concat_axis=0, tiled=True)
    e, sl, h, w = x.shape
    x = halo(x, "gy", 3, CH)
    x = halo(x, "gx", 2, RH)
    hp, wp = h + 2 * RH, w + 2 * CH
    x = jnp.transpose(x, (1, 2, 0, 3))
    r = kernel.shape[1]

    gi = lax.axis_index("gx")
    gj = lax.axis_index("gy")
    grow = gi * h + jnp.arange(hp) - RH
    rm = ((grow >= 0) & (grow < h * lax.axis_size("gx"))).astype(jnp.float32)
    gcol = gj * w + jnp.arange(wp) - CH
    cv = ((gcol >= 0) & (gcol < w * lax.axis_size("gy"))).astype(jnp.float32)
    cm = jnp.broadcast_to(cv[:, None], (wp, r))

    rows = TR + 2 * RH
    nt = h // TR
    flops = 2 * sl * nt * rows * wp * r * (e + 2 * 3 * r)
    out = pl.pallas_call(
        functools.partial(fit_kernel, wp),
        out_shape=jax.ShapeDtypeStruct((sl, h, w, r), jnp.float32),
        grid=(sl, nt),
        in_specs=[
            pl.BlockSpec((1, hp, e, wp), lambda s, t: (s, 0, 0, 0)),
            pl.BlockSpec((e, r), lambda s, t: (0, 0)),
            pl.BlockSpec((3 * r, r), lambda s, t: (0, 0)),
            pl.BlockSpec((1, r), lambda s, t: (0, 0)),
            pl.BlockSpec((1, r), lambda s, t: (0, 0)),
            pl.BlockSpec((wp, r), lambda s, t: (0, 0)),
            pl.BlockSpec(memory_space=pltpu.SMEM),
        ],
        out_specs=pl.BlockSpec((1, TR, w, r), lambda s, t: (s, t, 0, 0)),
        scratch_shapes=[
            pltpu.VMEM((rows * wp, r), jnp.float32),
            pltpu.VMEM((rows * wp, r), jnp.float32),
            pltpu.VMEM((rows * wp, r), jnp.float32),
            pltpu.VMEM((rows * wp, 3 * r), jnp.bfloat16),
            pltpu.VMEM(((rows - 2) * wp, r), jnp.float32),
        ],
        compiler_params=pltpu.CompilerParams(
            dimension_semantics=("arbitrary", "arbitrary"),
            vmem_limit_bytes=48 * 1024 * 1024,
        ),
        cost_estimate=pl.CostEstimate(
            flops=flops, transcendentals=0,
            bytes_accessed=sl * (hp * wp * e * 2 + h * w * r * 4),
        ),
    )(x, kb, g3, step[None, :], lam[None, :], cm, rm)
    return out


def solution(mesh):
    in_specs = (P("gy", None, "gx", None), P(), P())
    out_specs = P(None, "gx", "gy", None)
    return jax.shard_map(
        per_device, mesh=mesh, in_specs=in_specs, out_specs=out_specs, check_vma=False
    )
```

```python
import functools

import jax
import jax.numpy as jnp
from jax import lax
from jax.experimental import pallas as pl
from jax.experimental.pallas import tpu as pltpu
from jax.sharding import PartitionSpec as P

E = 64
ITERS = 3
RH = 2
CH = 4
TR = 16


def kernel_parts(rates, smoothing):
    times = 10.0 * (jnp.arange(E, dtype=jnp.float32) + 1.0)
    raw = jnp.exp(-times[:, None] * rates[None, :])
    kernel = raw / jnp.sqrt(jnp.sum(raw * raw, axis=0))[None, :]
    gram = jnp.dot(kernel.T, kernel, precision=lax.Precision.HIGHEST)
    rowsum = jnp.sum(gram, axis=1)
    lam = smoothing * rowsum
    step = 1.0 / (rowsum + 8.0 * lam)
    return (kernel, gram, lam, step)


def halo(cells, axis, dim, width):
    count = lax.axis_size(axis)
    head = lax.slice_in_dim(cells, 0, width, axis=dim)
    tail = lax.slice_in_dim(cells, cells.shape[dim] - width, cells.shape[dim], axis=dim)
    return jnp.concatenate(
        [
            lax.ppermute(tail, axis, [(i, i + 1) for i in range(count - 1)]),
            cells,
            lax.ppermute(head, axis, [(i + 1, i) for i in range(count - 1)]),
        ],
        axis=dim,
    )


def split3(f):
    return f.astype(jnp.bfloat16)


def fit_kernel(wp, x_ref, kb_ref, g3_ref, step_ref, lam_ref, cm_ref, rm_ref,
               o_ref, b_ref, f0_ref, f1_ref, f3_ref, m_ref):
    t = pl.program_id(1)
    rows = TR + 2 * RH
    n = rows * wp
    base = pl.multiple_of(t * (TR * wp), 16)
    step = step_ref[...]
    lam = lam_ref[...]
    cm = cm_ref[...]

    b = jnp.dot(x_ref[0, pl.ds(base, n), :], kb_ref[...],
                preferred_element_type=jnp.float32)
    b_ref[...] = b
    f0 = jnp.maximum(b * step, 0.0)
    f0_ref[...] = f0
    f3_ref[...] = split3(f0)

    def update(src_ref, q):
        o = pl.multiple_of(q * wp, 8)
        c = src_ref[pl.ds(o, wp), :]
        up = src_ref[pl.ds(o - wp, wp), :]
        dn = src_ref[pl.ds(o + wp, wp), :]
        lf = pltpu.roll(c, 1, 0)
        rt = pltpu.roll(c, wp - 1, 0)
        lap = 4.0 * c - up - dn - lf - rt
        m = m_ref[pl.ds(o - wp, wp), :]
        g = m - b_ref[pl.ds(o, wp), :] + lam * lap
        return jnp.maximum(c - step * g, 0.0)

    m_ref[...] = jnp.dot(f3_ref[pl.ds(wp, (rows - 2) * wp), :], g3_ref[...],
                         preferred_element_type=jnp.float32)

    def body1(q, carry):
        f1 = update(f0_ref, q) * (cm * rm_ref[t * TR + q])
        f1_ref[pl.ds(pl.multiple_of(q * wp, 8), wp), :] = f1
        return carry

    lax.fori_loop(1, rows - 1, body1, 0)
    f1_ref[pl.ds(0, wp), :] = jnp.zeros((wp, f1_ref.shape[1]), jnp.float32)
    f1_ref[pl.ds((rows - 1) * wp, wp), :] = jnp.zeros((wp, f1_ref.shape[1]), jnp.float32)

    f3_ref[...] = split3(f1_ref[...])
    m_ref[...] = jnp.dot(f3_ref[pl.ds(wp, (rows - 2) * wp), :], g3_ref[...],
                         preferred_element_type=jnp.float32)

    def body2(q, carry):
        f2 = update(f1_ref, q)
        f2 = pltpu.roll(f2, wp - CH, 0)
        o_ref[0, q - RH] = f2[: wp - 2 * CH]
        return carry

    lax.fori_loop(RH, rows - RH, body2, 0)


def per_device(images, rates, smoothing):
    kernel, gram, lam, step = kernel_parts(rates, smoothing)
    kb = kernel.astype(jnp.bfloat16)
    gh = gram.astype(jnp.bfloat16)
    g3 = gh
    x = lax.all_to_all(images, "gy", split_axis=3, concat_axis=0, tiled=True)
    e, sl, h, w = x.shape
    x = halo(x, "gy", 3, CH)
    x = halo(x, "gx", 2, RH)
    hp, wp = h + 2 * RH, w + 2 * CH
    x = jnp.transpose(x, (1, 2, 3, 0)).reshape(sl, hp * wp, e)
    r = kernel.shape[1]

    gi = lax.axis_index("gx")
    gj = lax.axis_index("gy")
    grow = gi * h + jnp.arange(hp) - RH
    rm = ((grow >= 0) & (grow < h * lax.axis_size("gx"))).astype(jnp.float32)
    gcol = gj * w + jnp.arange(wp) - CH
    cv = ((gcol >= 0) & (gcol < w * lax.axis_size("gy"))).astype(jnp.float32)
    cm = jnp.broadcast_to(cv[:, None], (wp, r))

    rows = TR + 2 * RH
    nt = h // TR
    flops = 2 * sl * nt * rows * wp * r * (e + 2 * r)
    out = pl.pallas_call(
        functools.partial(fit_kernel, wp),
        out_shape=jax.ShapeDtypeStruct((sl, h, w, r), jnp.float32),
        grid=(sl, nt),
        in_specs=[
            pl.BlockSpec((1, hp * wp, e), lambda s, t: (s, 0, 0)),
            pl.BlockSpec((e, r), lambda s, t: (0, 0)),
            pl.BlockSpec((r, r), lambda s, t: (0, 0)),
            pl.BlockSpec((1, r), lambda s, t: (0, 0)),
            pl.BlockSpec((1, r), lambda s, t: (0, 0)),
            pl.BlockSpec((wp, r), lambda s, t: (0, 0)),
            pl.BlockSpec(memory_space=pltpu.SMEM),
        ],
        out_specs=pl.BlockSpec((1, TR, w, r), lambda s, t: (s, t, 0, 0)),
        scratch_shapes=[
            pltpu.VMEM((rows * wp, r), jnp.float32),
            pltpu.VMEM((rows * wp, r), jnp.float32),
            pltpu.VMEM((rows * wp, r), jnp.float32),
            pltpu.VMEM((rows * wp, r), jnp.bfloat16),
            pltpu.VMEM(((rows - 2) * wp, r), jnp.float32),
        ],
        compiler_params=pltpu.CompilerParams(
            dimension_semantics=("arbitrary", "arbitrary"),
            vmem_limit_bytes=48 * 1024 * 1024,
        ),
        cost_estimate=pl.CostEstimate(
            flops=flops, transcendentals=0,
            bytes_accessed=sl * (hp * wp * e * 2 + h * w * r * 4),
        ),
    )(x, kb, g3, step[None, :], lam[None, :], cm, rm)
    return out


def solution(mesh):
    in_specs = (P("gy", None, "gx", None), P(), P())
    out_specs = P(None, "gx", "gy", None)
    return jax.shard_map(
        per_device, mesh=mesh, in_specs=in_specs, out_specs=out_specs, check_vma=False
    )
```

```python
import functools

import jax
import jax.numpy as jnp
from jax import lax
from jax.experimental import pallas as pl
from jax.experimental.pallas import tpu as pltpu
from jax.sharding import PartitionSpec as P

E = 64
ITERS = 3
RH = 2
CH = 4
TR = 16


def kernel_parts(rates, smoothing):
    times = 10.0 * (jnp.arange(E, dtype=jnp.float32) + 1.0)
    raw = jnp.exp(-times[:, None] * rates[None, :])
    kernel = raw / jnp.sqrt(jnp.sum(raw * raw, axis=0))[None, :]
    gram = jnp.dot(kernel.T, kernel, precision=lax.Precision.HIGHEST)
    rowsum = jnp.sum(gram, axis=1)
    lam = smoothing * rowsum
    step = 1.0 / (rowsum + 8.0 * lam)
    return (kernel, gram, lam, step)


def halo(cells, axis, dim, width):
    count = lax.axis_size(axis)
    head = lax.slice_in_dim(cells, 0, width, axis=dim)
    tail = lax.slice_in_dim(cells, cells.shape[dim] - width, cells.shape[dim], axis=dim)
    return jnp.concatenate(
        [
            lax.ppermute(tail, axis, [(i, i + 1) for i in range(count - 1)]),
            cells,
            lax.ppermute(head, axis, [(i + 1, i) for i in range(count - 1)]),
        ],
        axis=dim,
    )


def split3(f):
    return f.astype(jnp.bfloat16)


def fit_kernel(wp, bin_ref, g3_ref, step_ref, lam_ref, cm_ref, rm_ref,
               o_ref, b_ref, f0_ref, f1_ref, f3_ref, m_ref):
    t = pl.program_id(1)
    rows = TR + 2 * RH
    n = rows * wp
    base = pl.multiple_of(t * (TR * wp), 16)
    step = step_ref[...]
    lam = lam_ref[...]
    cm = cm_ref[...]

    b = bin_ref[0, pl.ds(base, n), :]
    b_ref[...] = b
    f0 = jnp.maximum(b * step, 0.0)
    f0_ref[...] = f0
    f3_ref[...] = split3(f0)

    def update(src_ref, q):
        o = pl.multiple_of(q * wp, 8)
        c = src_ref[pl.ds(o, wp), :]
        up = src_ref[pl.ds(o - wp, wp), :]
        dn = src_ref[pl.ds(o + wp, wp), :]
        lf = pltpu.roll(c, 1, 0)
        rt = pltpu.roll(c, wp - 1, 0)
        lap = 4.0 * c - up - dn - lf - rt
        m = m_ref[pl.ds(o - wp, wp), :]
        g = m - b_ref[pl.ds(o, wp), :] + lam * lap
        return jnp.maximum(c - step * g, 0.0)

    m_ref[...] = jnp.dot(f3_ref[pl.ds(wp, (rows - 2) * wp), :], g3_ref[...],
                         preferred_element_type=jnp.float32)

    def body1(q, carry):
        f1 = update(f0_ref, q) * (cm * rm_ref[t * TR + q])
        f1_ref[pl.ds(pl.multiple_of(q * wp, 8), wp), :] = f1
        return carry

    lax.fori_loop(1, rows - 1, body1, 0)
    f1_ref[pl.ds(0, wp), :] = jnp.zeros((wp, f1_ref.shape[1]), jnp.float32)
    f1_ref[pl.ds((rows - 1) * wp, wp), :] = jnp.zeros((wp, f1_ref.shape[1]), jnp.float32)

    f3_ref[...] = split3(f1_ref[...])
    m_ref[...] = jnp.dot(f3_ref[pl.ds(wp, (rows - 2) * wp), :], g3_ref[...],
                         preferred_element_type=jnp.float32)

    def body2(q, carry):
        f2 = update(f1_ref, q)
        f2 = pltpu.roll(f2, wp - CH, 0)
        o_ref[0, q - RH] = f2[: wp - 2 * CH]
        return carry

    lax.fori_loop(RH, rows - RH, body2, 0)


def per_device(images, rates, smoothing):
    kernel, gram, lam, step = kernel_parts(rates, smoothing)
    kb = kernel.astype(jnp.bfloat16)
    gh = gram.astype(jnp.bfloat16)
    g3 = gh
    x = lax.all_to_all(images, "gy", split_axis=3, concat_axis=0, tiled=True)
    e, sl, h, w = x.shape
    x = halo(x, "gy", 3, CH)
    x = halo(x, "gx", 2, RH)
    hp, wp = h + 2 * RH, w + 2 * CH
    bfull = jnp.einsum("esij,er->sijr", x, kb, preferred_element_type=jnp.float32)
    bfull = bfull.reshape(sl, hp * wp, kb.shape[1])
    r = kernel.shape[1]

    gi = lax.axis_index("gx")
    gj = lax.axis_index("gy")
    grow = gi * h + jnp.arange(hp) - RH
    rm = ((grow >= 0) & (grow < h * lax.axis_size("gx"))).astype(jnp.float32)
    gcol = gj * w + jnp.arange(wp) - CH
    cv = ((gcol >= 0) & (gcol < w * lax.axis_size("gy"))).astype(jnp.float32)
    cm = jnp.broadcast_to(cv[:, None], (wp, r))

    rows = TR + 2 * RH
    nt = h // TR
    flops = 2 * sl * nt * rows * wp * r * 2 * r
    out = pl.pallas_call(
        functools.partial(fit_kernel, wp),
        out_shape=jax.ShapeDtypeStruct((sl, h, w, r), jnp.float32),
        grid=(sl, nt),
        in_specs=[
            pl.BlockSpec((1, hp * wp, r), lambda s, t: (s, 0, 0)),
            pl.BlockSpec((r, r), lambda s, t: (0, 0)),
            pl.BlockSpec((1, r), lambda s, t: (0, 0)),
            pl.BlockSpec((1, r), lambda s, t: (0, 0)),
            pl.BlockSpec((wp, r), lambda s, t: (0, 0)),
            pl.BlockSpec(memory_space=pltpu.SMEM),
        ],
        out_specs=pl.BlockSpec((1, TR, w, r), lambda s, t: (s, t, 0, 0)),
        scratch_shapes=[
            pltpu.VMEM((rows * wp, r), jnp.float32),
            pltpu.VMEM((rows * wp, r), jnp.float32),
            pltpu.VMEM((rows * wp, r), jnp.float32),
            pltpu.VMEM((rows * wp, r), jnp.bfloat16),
            pltpu.VMEM(((rows - 2) * wp, r), jnp.float32),
        ],
        compiler_params=pltpu.CompilerParams(
            dimension_semantics=("arbitrary", "arbitrary"),
            vmem_limit_bytes=60 * 1024 * 1024,
        ),
        cost_estimate=pl.CostEstimate(
            flops=flops, transcendentals=0,
            bytes_accessed=sl * (hp * wp * r * 4 + h * w * r * 4),
        ),
    )(bfull, g3, step[None, :], lam[None, :], cm, rm)
    return out


def solution(mesh):
    in_specs = (P("gy", None, "gx", None), P(), P())
    out_specs = P(None, "gx", "gy", None)
    return jax.shard_map(
        per_device, mesh=mesh, in_specs=in_specs, out_specs=out_specs, check_vma=False
    )
```

```python
import functools

import jax
import jax.numpy as jnp
from jax import lax
from jax.experimental import pallas as pl
from jax.experimental.pallas import tpu as pltpu
from jax.sharding import PartitionSpec as P

E = 64
ITERS = 3
RH = 2
CH = 4
TR = 32


def kernel_parts(rates, smoothing):
    times = 10.0 * (jnp.arange(E, dtype=jnp.float32) + 1.0)
    raw = jnp.exp(-times[:, None] * rates[None, :])
    kernel = raw / jnp.sqrt(jnp.sum(raw * raw, axis=0))[None, :]
    gram = jnp.dot(kernel.T, kernel, precision=lax.Precision.HIGHEST)
    rowsum = jnp.sum(gram, axis=1)
    lam = smoothing * rowsum
    step = 1.0 / (rowsum + 8.0 * lam)
    return (kernel, gram, lam, step)


def halo(cells, axis, dim, width):
    count = lax.axis_size(axis)
    head = lax.slice_in_dim(cells, 0, width, axis=dim)
    tail = lax.slice_in_dim(cells, cells.shape[dim] - width, cells.shape[dim], axis=dim)
    return jnp.concatenate(
        [
            lax.ppermute(tail, axis, [(i, i + 1) for i in range(count - 1)]),
            cells,
            lax.ppermute(head, axis, [(i + 1, i) for i in range(count - 1)]),
        ],
        axis=dim,
    )


def split3(f):
    return f.astype(jnp.bfloat16)


def fit_kernel(wp, x_ref, kb_ref, g3_ref, step_ref, lam_ref, cm_ref, rm_ref,
               o_ref, b_ref, f0_ref, f1_ref, f3_ref, m_ref):
    t = pl.program_id(1)
    rows = TR + 2 * RH
    n = rows * wp
    base = pl.multiple_of(t * (TR * wp), 16)
    step = step_ref[...]
    lam = lam_ref[...]
    cm = cm_ref[...]

    b = jnp.dot(x_ref[0, pl.ds(base, n), :], kb_ref[...],
                preferred_element_type=jnp.float32)
    b_ref[...] = b
    f0 = jnp.maximum(b * step, 0.0)
    f0_ref[...] = f0
    f3_ref[...] = split3(f0)

    def update(src_ref, q):
        o = pl.multiple_of(q * wp, 8)
        c = src_ref[pl.ds(o, wp), :]
        up = src_ref[pl.ds(o - wp, wp), :]
        dn = src_ref[pl.ds(o + wp, wp), :]
        lf = pltpu.roll(c, 1, 0)
        rt = pltpu.roll(c, wp - 1, 0)
        lap = 4.0 * c - up - dn - lf - rt
        m = m_ref[pl.ds(o - wp, wp), :]
        g = m - b_ref[pl.ds(o, wp), :] + lam * lap
        return jnp.maximum(c - step * g, 0.0)

    m_ref[...] = jnp.dot(f3_ref[pl.ds(wp, (rows - 2) * wp), :], g3_ref[...],
                         preferred_element_type=jnp.float32)

    def body1(q, carry):
        f1 = update(f0_ref, q) * (cm * rm_ref[t * TR + q])
        f1_ref[pl.ds(pl.multiple_of(q * wp, 8), wp), :] = f1
        return carry

    lax.fori_loop(1, rows - 1, body1, 0)
    f1_ref[pl.ds(0, wp), :] = jnp.zeros((wp, f1_ref.shape[1]), jnp.float32)
    f1_ref[pl.ds((rows - 1) * wp, wp), :] = jnp.zeros((wp, f1_ref.shape[1]), jnp.float32)

    f3_ref[...] = split3(f1_ref[...])
    m_ref[...] = jnp.dot(f3_ref[pl.ds(wp, (rows - 2) * wp), :], g3_ref[...],
                         preferred_element_type=jnp.float32)

    def body2(q, carry):
        f2 = update(f1_ref, q)
        f2 = pltpu.roll(f2, wp - CH, 0)
        o_ref[0, q - RH] = f2[: wp - 2 * CH]
        return carry

    lax.fori_loop(RH, rows - RH, body2, 0)


def per_device(images, rates, smoothing):
    kernel, gram, lam, step = kernel_parts(rates, smoothing)
    kb = kernel.astype(jnp.bfloat16)
    gh = gram.astype(jnp.bfloat16)
    g3 = gh
    x = lax.all_to_all(images, "gy", split_axis=3, concat_axis=0, tiled=True)
    e, sl, h, w = x.shape
    x = halo(x, "gy", 3, CH)
    x = halo(x, "gx", 2, RH)
    hp, wp = h + 2 * RH, w + 2 * CH
    x = jnp.transpose(x, (1, 2, 3, 0)).reshape(sl, hp * wp, e)
    r = kernel.shape[1]

    gi = lax.axis_index("gx")
    gj = lax.axis_index("gy")
    grow = gi * h + jnp.arange(hp) - RH
    rm = ((grow >= 0) & (grow < h * lax.axis_size("gx"))).astype(jnp.float32)
    gcol = gj * w + jnp.arange(wp) - CH
    cv = ((gcol >= 0) & (gcol < w * lax.axis_size("gy"))).astype(jnp.float32)
    cm = jnp.broadcast_to(cv[:, None], (wp, r))

    rows = TR + 2 * RH
    nt = h // TR
    flops = 2 * sl * nt * rows * wp * r * (e + 2 * r)
    out = pl.pallas_call(
        functools.partial(fit_kernel, wp),
        out_shape=jax.ShapeDtypeStruct((sl, h, w, r), jnp.float32),
        grid=(sl, nt),
        in_specs=[
            pl.BlockSpec((1, hp * wp, e), lambda s, t: (s, 0, 0)),
            pl.BlockSpec((e, r), lambda s, t: (0, 0)),
            pl.BlockSpec((r, r), lambda s, t: (0, 0)),
            pl.BlockSpec((1, r), lambda s, t: (0, 0)),
            pl.BlockSpec((1, r), lambda s, t: (0, 0)),
            pl.BlockSpec((wp, r), lambda s, t: (0, 0)),
            pl.BlockSpec(memory_space=pltpu.SMEM),
        ],
        out_specs=pl.BlockSpec((1, TR, w, r), lambda s, t: (s, t, 0, 0)),
        scratch_shapes=[
            pltpu.VMEM((rows * wp, r), jnp.float32),
            pltpu.VMEM((rows * wp, r), jnp.float32),
            pltpu.VMEM((rows * wp, r), jnp.float32),
            pltpu.VMEM((rows * wp, r), jnp.bfloat16),
            pltpu.VMEM(((rows - 2) * wp, r), jnp.float32),
        ],
        compiler_params=pltpu.CompilerParams(
            dimension_semantics=("arbitrary", "arbitrary"),
            vmem_limit_bytes=48 * 1024 * 1024,
        ),
        cost_estimate=pl.CostEstimate(
            flops=flops, transcendentals=0,
            bytes_accessed=sl * (hp * wp * e * 2 + h * w * r * 4),
        ),
    )(x, kb, g3, step[None, :], lam[None, :], cm, rm)
    return out


def solution(mesh):
    in_specs = (P("gy", None, "gx", None), P(), P())
    out_specs = P(None, "gx", "gy", None)
    return jax.shard_map(
        per_device, mesh=mesh, in_specs=in_specs, out_specs=out_specs, check_vma=False
    )
```

```python
import functools

import jax
import jax.numpy as jnp
from jax import lax
from jax.experimental import pallas as pl
from jax.experimental.pallas import tpu as pltpu
from jax.sharding import PartitionSpec as P

E = 64
ITERS = 3
RH = 2
CH = 4
TR = 32


def kernel_parts(rates, smoothing):
    times = 10.0 * (jnp.arange(E, dtype=jnp.float32) + 1.0)
    raw = jnp.exp(-times[:, None] * rates[None, :])
    kernel = raw / jnp.sqrt(jnp.sum(raw * raw, axis=0))[None, :]
    gram = jnp.dot(kernel.T, kernel, precision=lax.Precision.HIGHEST)
    rowsum = jnp.sum(gram, axis=1)
    lam = smoothing * rowsum
    step = 1.0 / (rowsum + 8.0 * lam)
    return (kernel, gram, lam, step)


def halo(cells, axis, dim, width):
    count = lax.axis_size(axis)
    head = lax.slice_in_dim(cells, 0, width, axis=dim)
    tail = lax.slice_in_dim(cells, cells.shape[dim] - width, cells.shape[dim], axis=dim)
    return jnp.concatenate(
        [
            lax.ppermute(tail, axis, [(i, i + 1) for i in range(count - 1)]),
            cells,
            lax.ppermute(head, axis, [(i + 1, i) for i in range(count - 1)]),
        ],
        axis=dim,
    )


def split3(f):
    return f.astype(jnp.bfloat16)


def fit_kernel(wp, x_ref, kb_ref, g3_ref, step_ref, lam_ref, cm_ref, rm_ref,
               o_ref, b_ref, f0_ref, f1_ref, f3_ref, m_ref):
    t = pl.program_id(1)
    rows = TR + 2 * RH
    n = rows * wp
    base = pl.multiple_of(t * (TR * wp), 16)
    step = step_ref[...]
    lam = lam_ref[...]
    cm = cm_ref[...]

    b = jnp.dot(x_ref[0, pl.ds(base, n), :], kb_ref[...],
                preferred_element_type=jnp.float32)
    b_ref[...] = b
    f0 = jnp.maximum(b * step, 0.0)
    f0_ref[...] = f0
    f3_ref[...] = split3(f0)

    def update(src_ref, q):
        o = pl.multiple_of(q * wp, 8)
        c = src_ref[pl.ds(o, wp), :]
        up = src_ref[pl.ds(o - wp, wp), :]
        dn = src_ref[pl.ds(o + wp, wp), :]
        lf = pltpu.roll(c, 1, 0)
        rt = pltpu.roll(c, wp - 1, 0)
        lap = 4.0 * c - up - dn - lf - rt
        m = m_ref[pl.ds(o - wp, wp), :]
        g = m - b_ref[pl.ds(o, wp), :] + lam * lap
        return jnp.maximum(c - step * g, 0.0)

    m_ref[...] = jnp.dot(f3_ref[pl.ds(wp, (rows - 2) * wp), :], g3_ref[...],
                         preferred_element_type=jnp.float32)

    def body1(q, carry):
        f1 = update(f0_ref, q) * (cm * rm_ref[t * TR + q])
        f1_ref[pl.ds(pl.multiple_of(q * wp, 8), wp), :] = f1
        return carry

    lax.fori_loop(1, rows - 1, body1, 0)
    f1_ref[pl.ds(0, wp), :] = jnp.zeros((wp, f1_ref.shape[1]), jnp.float32)
    f1_ref[pl.ds((rows - 1) * wp, wp), :] = jnp.zeros((wp, f1_ref.shape[1]), jnp.float32)

    f3_ref[...] = split3(f1_ref[...])
    m_ref[...] = jnp.dot(f3_ref[pl.ds(wp, (rows - 2) * wp), :], g3_ref[...],
                         preferred_element_type=jnp.float32)

    def body2(q, carry):
        f2 = update(f1_ref, q)
        f2 = pltpu.roll(f2, wp - CH, 0)
        o_ref[0, q - RH] = f2[: wp - 2 * CH]
        return carry

    lax.fori_loop(RH, rows - RH, body2, 0)


def per_device(images, rates, smoothing):
    kernel, gram, lam, step = kernel_parts(rates, smoothing)
    kb = kernel.astype(jnp.bfloat16)
    gh = gram.astype(jnp.bfloat16)
    g3 = gh
    ny = lax.axis_size("gy")
    e = images.shape[0] * ny
    sl, h = images.shape[1], images.shape[2]
    w = images.shape[3] // ny
    hp, wp = h + 2 * RH, w + 2 * CH
    x = halo(images, "gx", 2, RH)
    x = jnp.pad(x, ((0, 0), (0, 0), (0, 0), (CH, CH)))
    x = jnp.stack([x[..., j * w: j * w + wp] for j in range(ny)], axis=3)
    x = lax.all_to_all(x, "gy", split_axis=3, concat_axis=0, tiled=True)
    x = x.reshape(e, sl, hp, wp)
    x = jnp.transpose(x, (1, 2, 3, 0)).reshape(sl, hp * wp, e)
    r = kernel.shape[1]

    gi = lax.axis_index("gx")
    gj = lax.axis_index("gy")
    grow = gi * h + jnp.arange(hp) - RH
    rm = ((grow >= 0) & (grow < h * lax.axis_size("gx"))).astype(jnp.float32)
    gcol = gj * w + jnp.arange(wp) - CH
    cv = ((gcol >= 0) & (gcol < w * lax.axis_size("gy"))).astype(jnp.float32)
    cm = jnp.broadcast_to(cv[:, None], (wp, r))

    rows = TR + 2 * RH
    nt = h // TR
    flops = 2 * sl * nt * rows * wp * r * (e + 2 * r)
    out = pl.pallas_call(
        functools.partial(fit_kernel, wp),
        out_shape=jax.ShapeDtypeStruct((sl, h, w, r), jnp.float32),
        grid=(sl, nt),
        in_specs=[
            pl.BlockSpec((1, hp * wp, e), lambda s, t: (s, 0, 0)),
            pl.BlockSpec((e, r), lambda s, t: (0, 0)),
            pl.BlockSpec((r, r), lambda s, t: (0, 0)),
            pl.BlockSpec((1, r), lambda s, t: (0, 0)),
            pl.BlockSpec((1, r), lambda s, t: (0, 0)),
            pl.BlockSpec((wp, r), lambda s, t: (0, 0)),
            pl.BlockSpec(memory_space=pltpu.SMEM),
        ],
        out_specs=pl.BlockSpec((1, TR, w, r), lambda s, t: (s, t, 0, 0)),
        scratch_shapes=[
            pltpu.VMEM((rows * wp, r), jnp.float32),
            pltpu.VMEM((rows * wp, r), jnp.float32),
            pltpu.VMEM((rows * wp, r), jnp.float32),
            pltpu.VMEM((rows * wp, r), jnp.bfloat16),
            pltpu.VMEM(((rows - 2) * wp, r), jnp.float32),
        ],
        compiler_params=pltpu.CompilerParams(
            dimension_semantics=("arbitrary", "arbitrary"),
            vmem_limit_bytes=48 * 1024 * 1024,
        ),
        cost_estimate=pl.CostEstimate(
            flops=flops, transcendentals=0,
            bytes_accessed=sl * (hp * wp * e * 2 + h * w * r * 4),
        ),
    )(x, kb, g3, step[None, :], lam[None, :], cm, rm)
    return out


def solution(mesh):
    in_specs = (P("gy", None, "gx", None), P(), P())
    out_specs = P(None, "gx", "gy", None)
    return jax.shard_map(
        per_device, mesh=mesh, in_specs=in_specs, out_specs=out_specs, check_vma=False
    )
```

```python
import functools

import jax
import jax.numpy as jnp
from jax import lax
from jax.experimental import pallas as pl
from jax.experimental.pallas import tpu as pltpu
from jax.sharding import PartitionSpec as P

E = 64
ITERS = 3
RH = 2
CH = 4
TR = 32


def kernel_parts(rates, smoothing):
    times = 10.0 * (jnp.arange(E, dtype=jnp.float32) + 1.0)
    raw = jnp.exp(-times[:, None] * rates[None, :])
    kernel = raw / jnp.sqrt(jnp.sum(raw * raw, axis=0))[None, :]
    gram = jnp.dot(kernel.T, kernel, precision=lax.Precision.HIGHEST)
    rowsum = jnp.sum(gram, axis=1)
    lam = smoothing * rowsum
    step = 1.0 / (rowsum + 8.0 * lam)
    return (kernel, gram, lam, step)


def halo(cells, axis, dim, width):
    count = lax.axis_size(axis)
    head = lax.slice_in_dim(cells, 0, width, axis=dim)
    tail = lax.slice_in_dim(cells, cells.shape[dim] - width, cells.shape[dim], axis=dim)
    return jnp.concatenate(
        [
            lax.ppermute(tail, axis, [(i, i + 1) for i in range(count - 1)]),
            cells,
            lax.ppermute(head, axis, [(i + 1, i) for i in range(count - 1)]),
        ],
        axis=dim,
    )


def split3(f):
    return f.astype(jnp.bfloat16)


def fit_kernel(wp, x_ref, kb_ref, g3_ref, step_ref, lam_ref, cm_ref, rm_ref,
               o_ref, b_ref, f0_ref, f1_ref, f3_ref, m_ref):
    t = pl.program_id(1)
    rows = TR + 2 * RH
    n = rows * wp
    base = pl.multiple_of(t * (TR * wp), 16)
    step = step_ref[...]
    lam = lam_ref[...]
    cm = cm_ref[...]

    b = jnp.dot(x_ref[0, pl.ds(base, n), :], kb_ref[...],
                preferred_element_type=jnp.float32)
    b_ref[...] = b
    f0 = jnp.maximum(b * step, 0.0)
    f0_ref[...] = f0
    f3_ref[...] = split3(f0)

    def update(src_ref, q):
        o = pl.multiple_of(q * wp, 8)
        c = src_ref[pl.ds(o, wp), :]
        up = src_ref[pl.ds(o - wp, wp), :]
        dn = src_ref[pl.ds(o + wp, wp), :]
        lf = pltpu.roll(c, 1, 0)
        rt = pltpu.roll(c, wp - 1, 0)
        lap = 4.0 * c - up - dn - lf - rt
        m = m_ref[pl.ds(o - wp, wp), :]
        g = m - b_ref[pl.ds(o, wp), :] + lam * lap
        return jnp.maximum(c - step * g, 0.0)

    m_ref[...] = jnp.dot(f3_ref[pl.ds(wp, (rows - 2) * wp), :], g3_ref[...],
                         preferred_element_type=jnp.float32)

    def body1(q, carry):
        f1 = update(f0_ref, q) * (cm * rm_ref[t * TR + q])
        f1_ref[pl.ds(pl.multiple_of(q * wp, 8), wp), :] = f1
        return carry

    lax.fori_loop(1, rows - 1, body1, 0)
    f1_ref[pl.ds(0, wp), :] = jnp.zeros((wp, f1_ref.shape[1]), jnp.float32)
    f1_ref[pl.ds((rows - 1) * wp, wp), :] = jnp.zeros((wp, f1_ref.shape[1]), jnp.float32)

    f3_ref[...] = split3(f1_ref[...])
    m_ref[...] = jnp.dot(f3_ref[pl.ds(wp, (rows - 2) * wp), :], g3_ref[...],
                         preferred_element_type=jnp.float32)

    def body2(q, carry):
        f2 = update(f1_ref, q)
        f2 = pltpu.roll(f2, wp - CH, 0)
        o_ref[0, q - RH] = f2[: wp - 2 * CH]
        return carry

    lax.fori_loop(RH, rows - RH, body2, 0)


def per_device(images, rates, smoothing):
    kernel, gram, lam, step = kernel_parts(rates, smoothing)
    kb = kernel.astype(jnp.bfloat16)
    gh = gram.astype(jnp.bfloat16)
    g3 = gh
    ny = lax.axis_size("gy")
    ee = images.shape[0]
    e = ee * ny
    sl, h = images.shape[1], images.shape[2]
    w = images.shape[3] // ny
    hp, wp = h + 2 * RH, w + 2 * CH
    x = halo(images, "gx", 2, RH)
    x = jnp.pad(x, ((0, 0), (0, 0), (0, 0), (CH, CH)))
    mid = x[..., CH:CH + ny * w].reshape(ee, sl, hp, ny, w)
    left = x[..., 0:ny * w].reshape(ee, sl, hp, ny, w)[..., :CH]
    right = x[..., 2 * CH:2 * CH + ny * w].reshape(ee, sl, hp, ny, w)[..., w - CH:]
    x = jnp.concatenate([left, mid, right], axis=4)
    x = jnp.transpose(x, (0, 1, 3, 2, 4)).reshape(ee, sl, ny, hp * wp)
    x = lax.all_to_all(x, "gy", split_axis=2, concat_axis=0, tiled=True)
    x = jnp.transpose(x.reshape(e, sl, hp * wp), (1, 2, 0))
    r = kernel.shape[1]

    gi = lax.axis_index("gx")
    gj = lax.axis_index("gy")
    grow = gi * h + jnp.arange(hp) - RH
    rm = ((grow >= 0) & (grow < h * lax.axis_size("gx"))).astype(jnp.float32)
    gcol = gj * w + jnp.arange(wp) - CH
    cv = ((gcol >= 0) & (gcol < w * lax.axis_size("gy"))).astype(jnp.float32)
    cm = jnp.broadcast_to(cv[:, None], (wp, r))

    rows = TR + 2 * RH
    nt = h // TR
    flops = 2 * sl * nt * rows * wp * r * (e + 2 * r)
    out = pl.pallas_call(
        functools.partial(fit_kernel, wp),
        out_shape=jax.ShapeDtypeStruct((sl, h, w, r), jnp.float32),
        grid=(sl, nt),
        in_specs=[
            pl.BlockSpec((1, hp * wp, e), lambda s, t: (s, 0, 0)),
            pl.BlockSpec((e, r), lambda s, t: (0, 0)),
            pl.BlockSpec((r, r), lambda s, t: (0, 0)),
            pl.BlockSpec((1, r), lambda s, t: (0, 0)),
            pl.BlockSpec((1, r), lambda s, t: (0, 0)),
            pl.BlockSpec((wp, r), lambda s, t: (0, 0)),
            pl.BlockSpec(memory_space=pltpu.SMEM),
        ],
        out_specs=pl.BlockSpec((1, TR, w, r), lambda s, t: (s, t, 0, 0)),
        scratch_shapes=[
            pltpu.VMEM((rows * wp, r), jnp.float32),
            pltpu.VMEM((rows * wp, r), jnp.float32),
            pltpu.VMEM((rows * wp, r), jnp.float32),
            pltpu.VMEM((rows * wp, r), jnp.bfloat16),
            pltpu.VMEM(((rows - 2) * wp, r), jnp.float32),
        ],
        compiler_params=pltpu.CompilerParams(
            dimension_semantics=("arbitrary", "arbitrary"),
            vmem_limit_bytes=48 * 1024 * 1024,
        ),
        cost_estimate=pl.CostEstimate(
            flops=flops, transcendentals=0,
            bytes_accessed=sl * (hp * wp * e * 2 + h * w * r * 4),
        ),
    )(x, kb, g3, step[None, :], lam[None, :], cm, rm)
    return out


def solution(mesh):
    in_specs = (P("gy", None, "gx", None), P(), P())
    out_specs = P(None, "gx", "gy", None)
    return jax.shard_map(
        per_device, mesh=mesh, in_specs=in_specs, out_specs=out_specs, check_vma=False
    )
```

```python
import functools

import jax
import jax.numpy as jnp
from jax import lax
from jax.experimental import pallas as pl
from jax.experimental.pallas import tpu as pltpu
from jax.sharding import PartitionSpec as P

E = 64
ITERS = 3
RH = 2
CH = 4
TR = 32


def kernel_parts(rates, smoothing):
    times = 10.0 * (jnp.arange(E, dtype=jnp.float32) + 1.0)
    raw = jnp.exp(-times[:, None] * rates[None, :])
    kernel = raw / jnp.sqrt(jnp.sum(raw * raw, axis=0))[None, :]
    gram = jnp.dot(kernel.T, kernel, precision=lax.Precision.HIGHEST)
    rowsum = jnp.sum(gram, axis=1)
    lam = smoothing * rowsum
    step = 1.0 / (rowsum + 8.0 * lam)
    return (kernel, gram, lam, step)


def halo(cells, axis, dim, width):
    count = lax.axis_size(axis)
    head = lax.slice_in_dim(cells, 0, width, axis=dim)
    tail = lax.slice_in_dim(cells, cells.shape[dim] - width, cells.shape[dim], axis=dim)
    return jnp.concatenate(
        [
            lax.ppermute(tail, axis, [(i, i + 1) for i in range(count - 1)]),
            cells,
            lax.ppermute(head, axis, [(i + 1, i) for i in range(count - 1)]),
        ],
        axis=dim,
    )


def split3(f):
    return f.astype(jnp.bfloat16)


def fit_kernel(wp, aliased, x_ref, kb_ref, g3_ref, step_ref, lam_ref, cm_ref, rm_ref,
               *rest):
    if aliased:
        rest = rest[1:]
    o_ref, b_ref, f0_ref, f1_ref, f3_ref, m_ref = rest
    t = pl.program_id(0)
    rows = TR + 2 * RH
    n = rows * wp
    base = pl.multiple_of(t * (TR * wp), 16)
    step = step_ref[...]
    lam = lam_ref[...]
    cm = cm_ref[...]

    b = jnp.dot(x_ref[0, pl.ds(base, n), :], kb_ref[...],
                preferred_element_type=jnp.float32)
    b_ref[...] = b
    f0 = jnp.maximum(b * step, 0.0)
    f0_ref[...] = f0
    f3_ref[...] = split3(f0)

    def update(src_ref, q):
        o = pl.multiple_of(q * wp, 8)
        c = src_ref[pl.ds(o, wp), :]
        up = src_ref[pl.ds(o - wp, wp), :]
        dn = src_ref[pl.ds(o + wp, wp), :]
        lf = pltpu.roll(c, 1, 0)
        rt = pltpu.roll(c, wp - 1, 0)
        lap = 4.0 * c - up - dn - lf - rt
        m = m_ref[pl.ds(o - wp, wp), :]
        g = m - b_ref[pl.ds(o, wp), :] + lam * lap
        return jnp.maximum(c - step * g, 0.0)

    m_ref[...] = jnp.dot(f3_ref[pl.ds(wp, (rows - 2) * wp), :], g3_ref[...],
                         preferred_element_type=jnp.float32)

    def body1(q, carry):
        f1 = update(f0_ref, q) * (cm * rm_ref[t * TR + q])
        f1_ref[pl.ds(pl.multiple_of(q * wp, 8), wp), :] = f1
        return carry

    lax.fori_loop(1, rows - 1, body1, 0)
    f1_ref[pl.ds(0, wp), :] = jnp.zeros((wp, f1_ref.shape[1]), jnp.float32)
    f1_ref[pl.ds((rows - 1) * wp, wp), :] = jnp.zeros((wp, f1_ref.shape[1]), jnp.float32)

    f3_ref[...] = split3(f1_ref[...])
    m_ref[...] = jnp.dot(f3_ref[pl.ds(wp, (rows - 2) * wp), :], g3_ref[...],
                         preferred_element_type=jnp.float32)

    def body2(q, carry):
        f2 = update(f1_ref, q)
        f2 = pltpu.roll(f2, wp - CH, 0)
        o_ref[0, q - RH] = f2[: wp - 2 * CH]
        return carry

    lax.fori_loop(RH, rows - RH, body2, 0)


def per_device(images, rates, smoothing):
    kernel, gram, lam, step = kernel_parts(rates, smoothing)
    kb = kernel.astype(jnp.bfloat16)
    gh = gram.astype(jnp.bfloat16)
    g3 = gh
    e = images.shape[0] * lax.axis_size("gy")
    sl, h = images.shape[1], images.shape[2]
    w = images.shape[3] // lax.axis_size("gy")
    hp, wp = h + 2 * RH, w + 2 * CH
    r = kernel.shape[1]

    gi = lax.axis_index("gx")
    gj = lax.axis_index("gy")
    grow = gi * h + jnp.arange(hp) - RH
    rm = ((grow >= 0) & (grow < h * lax.axis_size("gx"))).astype(jnp.float32)
    gcol = gj * w + jnp.arange(wp) - CH
    cv = ((gcol >= 0) & (gcol < w * lax.axis_size("gy"))).astype(jnp.float32)
    cm = jnp.broadcast_to(cv[:, None], (wp, r))

    rows = TR + 2 * RH
    nt = h // TR
    flops = 2 * nt * rows * wp * r * (e + 2 * r)
    out = None
    xs = None
    for s in range(sl):
        piece = images[:, s]
        if xs is not None:
            xs, piece = lax.optimization_barrier((xs, piece))
        x = lax.all_to_all(piece, "gy", split_axis=2, concat_axis=0, tiled=True)
        if out is not None:
            out, x = lax.optimization_barrier((out, x))
        x = halo(x, "gy", 2, CH)
        x = halo(x, "gx", 1, RH)
        x = jnp.transpose(x, (1, 2, 0)).reshape(1, hp * wp, e)
        xs = x
        args = [x, kb, g3, step[None, :], lam[None, :], cm, rm]
        in_specs = [
            pl.BlockSpec((1, hp * wp, e), lambda t: (0, 0, 0)),
            pl.BlockSpec((e, r), lambda t: (0, 0)),
            pl.BlockSpec((r, r), lambda t: (0, 0)),
            pl.BlockSpec((1, r), lambda t: (0, 0)),
            pl.BlockSpec((1, r), lambda t: (0, 0)),
            pl.BlockSpec((wp, r), lambda t: (0, 0)),
            pl.BlockSpec(memory_space=pltpu.SMEM),
        ]
        aliases = {}
        if out is not None:
            args.append(out)
            in_specs.append(pl.BlockSpec(memory_space=pl.ANY))
            aliases = {len(args) - 1: 0}
        out = pl.pallas_call(
            functools.partial(fit_kernel, wp, out is not None),
            out_shape=jax.ShapeDtypeStruct((sl, h, w, r), jnp.float32),
            grid=(nt,),
            in_specs=in_specs,
            out_specs=pl.BlockSpec((1, TR, w, r), lambda t, s=s: (s, t, 0, 0)),
            scratch_shapes=[
                pltpu.VMEM((rows * wp, r), jnp.float32),
                pltpu.VMEM((rows * wp, r), jnp.float32),
                pltpu.VMEM((rows * wp, r), jnp.float32),
                pltpu.VMEM((rows * wp, r), jnp.bfloat16),
                pltpu.VMEM(((rows - 2) * wp, r), jnp.float32),
            ],
            input_output_aliases=aliases,
            compiler_params=pltpu.CompilerParams(
                dimension_semantics=("arbitrary",),
                vmem_limit_bytes=48 * 1024 * 1024,
            ),
            cost_estimate=pl.CostEstimate(
                flops=flops, transcendentals=0,
                bytes_accessed=hp * wp * e * 2 + h * w * r * 4,
            ),
        )(*args)
    return out


def solution(mesh):
    in_specs = (P("gy", None, "gx", None), P(), P())
    out_specs = P(None, "gx", "gy", None)
    return jax.shard_map(
        per_device, mesh=mesh, in_specs=in_specs, out_specs=out_specs, check_vma=False
    )
```

```python
import functools

import jax
import jax.numpy as jnp
from jax import lax
from jax.experimental import pallas as pl
from jax.experimental.pallas import tpu as pltpu
from jax.sharding import PartitionSpec as P

E = 64
ITERS = 3
RH = 2
CH = 4
TR = 32


def kernel_parts(rates, smoothing):
    times = 10.0 * (jnp.arange(E, dtype=jnp.float32) + 1.0)
    raw = jnp.exp(-times[:, None] * rates[None, :])
    kernel = raw / jnp.sqrt(jnp.sum(raw * raw, axis=0))[None, :]
    gram = jnp.dot(kernel.T, kernel, precision=lax.Precision.HIGHEST)
    rowsum = jnp.sum(gram, axis=1)
    lam = smoothing * rowsum
    step = 1.0 / (rowsum + 8.0 * lam)
    return (kernel, gram, lam, step)


def halo(cells, axis, dim, width):
    count = lax.axis_size(axis)
    head = lax.slice_in_dim(cells, 0, width, axis=dim)
    tail = lax.slice_in_dim(cells, cells.shape[dim] - width, cells.shape[dim], axis=dim)
    return jnp.concatenate(
        [
            lax.ppermute(tail, axis, [(i, i + 1) for i in range(count - 1)]),
            cells,
            lax.ppermute(head, axis, [(i + 1, i) for i in range(count - 1)]),
        ],
        axis=dim,
    )


def fit_kernel(wp, x_ref, kb_ref, g_ref, step_ref, lam_ref, cm_ref, rm_ref,
               o_ref, b_ref, f1_ref, fb_ref, m_ref):
    t = pl.program_id(1)
    rows = TR + 2 * RH
    n = rows * wp
    r = b_ref.shape[1]
    base = pl.multiple_of(t * (TR * wp), 16)
    step = step_ref[...]
    lam = lam_ref[...]
    cm = cm_ref[...]

    b_ref[...] = jnp.dot(x_ref[0, pl.ds(base, n), :], kb_ref[...],
                         preferred_element_type=jnp.float32)
    inner = (rows - 2) * wp
    fb_ref[pl.ds(2 * wp, inner), :] = jnp.maximum(
        b_ref[pl.ds(wp, inner), :] * step, 0.0).astype(jnp.bfloat16)

    def lap_of(c, up, dn):
        lf = pltpu.roll(c, 1, 0)
        rt = pltpu.roll(c, wp - 1, 0)
        return 4.0 * c - up - dn - lf - rt

    def row1(q):
        o = q * wp
        bu = b_ref[pl.ds(o - wp, wp), :]
        bc = b_ref[pl.ds(o, wp), :]
        bd = b_ref[pl.ds(o + wp, wp), :]
        c = jnp.maximum(bc * step, 0.0)
        up = jnp.maximum(bu * step, 0.0)
        dn = jnp.maximum(bd * step, 0.0)
        g = m_ref[pl.ds(o - wp, wp), :] - bc + lam * lap_of(c, up, dn)
        return jnp.maximum(c - step * g, 0.0) * (cm * rm_ref[t * TR + q])

    m_ref[...] = jnp.dot(fb_ref[pl.ds(2 * wp, inner), :], g_ref[...],
                         preferred_element_type=jnp.float32)

    def body1(k, carry):
        q = 2 * k + 1
        pair = jnp.concatenate([row1(q), row1(q + 1)], axis=0)
        o = pl.multiple_of((q + 1) * wp, 16)
        f1_ref[pl.ds(o, 2 * wp), :] = pair
        fb_ref[pl.ds(o, 2 * wp), :] = pair.astype(jnp.bfloat16)
        return carry

    lax.fori_loop(0, (rows - 2) // 2, body1, 0)

    m_ref[...] = jnp.dot(fb_ref[pl.ds(2 * wp, inner), :], g_ref[...],
                         preferred_element_type=jnp.float32)

    def body2(q, carry):
        o = q * wp
        c = f1_ref[pl.ds(o + wp, wp), :]
        up = f1_ref[pl.ds(o, wp), :]
        dn = f1_ref[pl.ds(o + 2 * wp, wp), :]
        g = (m_ref[pl.ds(o - wp, wp), :] - b_ref[pl.ds(o, wp), :]
             + lam * lap_of(c, up, dn))
        f2 = jnp.maximum(c - step * g, 0.0)
        f2 = pltpu.roll(f2, wp - CH, 0)
        o_ref[0, q - RH] = f2[: wp - 2 * CH]
        return carry

    lax.fori_loop(RH, rows - RH, body2, 0)


def per_device(images, rates, smoothing):
    kernel, gram, lam, step = kernel_parts(rates, smoothing)
    kb = kernel.astype(jnp.bfloat16)
    gh = gram.astype(jnp.bfloat16)
    g3 = gh
    x = lax.all_to_all(images, "gy", split_axis=3, concat_axis=0, tiled=True)
    e, sl, h, w = x.shape
    x = halo(x, "gy", 3, CH)
    x = halo(x, "gx", 2, RH)
    hp, wp = h + 2 * RH, w + 2 * CH
    x = jnp.transpose(x, (1, 2, 3, 0)).reshape(sl, hp * wp, e)
    r = kernel.shape[1]

    gi = lax.axis_index("gx")
    gj = lax.axis_index("gy")
    grow = gi * h + jnp.arange(hp) - RH
    rm = ((grow >= 0) & (grow < h * lax.axis_size("gx"))).astype(jnp.float32)
    gcol = gj * w + jnp.arange(wp) - CH
    cv = ((gcol >= 0) & (gcol < w * lax.axis_size("gy"))).astype(jnp.float32)
    cm = jnp.broadcast_to(cv[:, None], (wp, r))

    rows = TR + 2 * RH
    nt = h // TR
    flops = 2 * sl * nt * rows * wp * r * (e + 2 * r)
    out = pl.pallas_call(
        functools.partial(fit_kernel, wp),
        out_shape=jax.ShapeDtypeStruct((sl, h, w, r), jnp.float32),
        grid=(sl, nt),
        in_specs=[
            pl.BlockSpec((1, hp * wp, e), lambda s, t: (s, 0, 0)),
            pl.BlockSpec((e, r), lambda s, t: (0, 0)),
            pl.BlockSpec((r, r), lambda s, t: (0, 0)),
            pl.BlockSpec((1, r), lambda s, t: (0, 0)),
            pl.BlockSpec((1, r), lambda s, t: (0, 0)),
            pl.BlockSpec((wp, r), lambda s, t: (0, 0)),
            pl.BlockSpec(memory_space=pltpu.SMEM),
        ],
        out_specs=pl.BlockSpec((1, TR, w, r), lambda s, t: (s, t, 0, 0)),
        scratch_shapes=[
            pltpu.VMEM((rows * wp, r), jnp.float32),
            pltpu.VMEM(((rows + 2) * wp, r), jnp.float32),
            pltpu.VMEM(((rows + 2) * wp, r), jnp.bfloat16),
            pltpu.VMEM(((rows - 2) * wp, r), jnp.float32),
        ],
        compiler_params=pltpu.CompilerParams(
            dimension_semantics=("arbitrary", "arbitrary"),
            vmem_limit_bytes=48 * 1024 * 1024,
        ),
        cost_estimate=pl.CostEstimate(
            flops=flops, transcendentals=0,
            bytes_accessed=sl * (hp * wp * e * 2 + h * w * r * 4),
        ),
    )(x, kb, g3, step[None, :], lam[None, :], cm, rm)
    return out


def solution(mesh):
    in_specs = (P("gy", None, "gx", None), P(), P())
    out_specs = P(None, "gx", "gy", None)
    return jax.shard_map(
        per_device, mesh=mesh, in_specs=in_specs, out_specs=out_specs, check_vma=False
    )
```

```python
import functools

import jax
import jax.numpy as jnp
from jax import lax
from jax.experimental import pallas as pl
from jax.experimental.pallas import tpu as pltpu
from jax.sharding import PartitionSpec as P

E = 64
ITERS = 3
RH = 2
CH = 4
TR = 32


def kernel_parts(rates, smoothing):
    times = 10.0 * (jnp.arange(E, dtype=jnp.float32) + 1.0)
    raw = jnp.exp(-times[:, None] * rates[None, :])
    kernel = raw / jnp.sqrt(jnp.sum(raw * raw, axis=0))[None, :]
    gram = jnp.dot(kernel.T, kernel, precision=lax.Precision.HIGHEST)
    rowsum = jnp.sum(gram, axis=1)
    lam = smoothing * rowsum
    step = 1.0 / (rowsum + 8.0 * lam)
    return (kernel, gram, lam, step)


def halo(cells, axis, dim, width):
    count = lax.axis_size(axis)
    head = lax.slice_in_dim(cells, 0, width, axis=dim)
    tail = lax.slice_in_dim(cells, cells.shape[dim] - width, cells.shape[dim], axis=dim)
    return jnp.concatenate(
        [
            lax.ppermute(tail, axis, [(i, i + 1) for i in range(count - 1)]),
            cells,
            lax.ppermute(head, axis, [(i + 1, i) for i in range(count - 1)]),
        ],
        axis=dim,
    )


def fit_kernel(wp, x_ref, kb_ref, g3_ref, step_ref, alpha_ref, beta_ref, cm_ref, rm_ref,
               o_ref, b_ref, f0_ref, f1_ref, f3_ref, m_ref):
    t = pl.program_id(1)
    rows = TR + 2 * RH
    n = rows * wp
    base = pl.multiple_of(t * (TR * wp), 16)
    step = step_ref[...]
    alpha = alpha_ref[...]
    beta = beta_ref[...]
    cm = cm_ref[...]

    sb = jnp.dot(x_ref[0, pl.ds(base, n), :], kb_ref[...],
                 preferred_element_type=jnp.float32) * step
    b_ref[...] = sb
    f0 = jnp.maximum(sb, 0.0)
    f0_ref[...] = f0
    f3_ref[...] = f0.astype(jnp.bfloat16)

    def update(src_ref, q):
        o = pl.multiple_of(q * wp, 8)
        c = src_ref[pl.ds(o, wp), :]
        up = src_ref[pl.ds(o - wp, wp), :]
        dn = src_ref[pl.ds(o + wp, wp), :]
        lf = pltpu.roll(c, 1, 0)
        rt = pltpu.roll(c, wp - 1, 0)
        nb = (up + dn) + (lf + rt)
        v = (alpha * c + beta * nb) + (b_ref[pl.ds(o, wp), :] - m_ref[pl.ds(o - wp, wp), :])
        return jnp.maximum(v, 0.0)

    m_ref[...] = jnp.dot(f3_ref[pl.ds(wp, (rows - 2) * wp), :], g3_ref[...],
                         preferred_element_type=jnp.float32)

    def body1(q, carry):
        f1 = update(f0_ref, q) * (cm * rm_ref[t * TR + q])
        f1_ref[pl.ds(pl.multiple_of(q * wp, 8), wp), :] = f1
        return carry

    lax.fori_loop(1, rows - 1, body1, 0)
    f1_ref[pl.ds(0, wp), :] = jnp.zeros((wp, f1_ref.shape[1]), jnp.float32)
    f1_ref[pl.ds((rows - 1) * wp, wp), :] = jnp.zeros((wp, f1_ref.shape[1]), jnp.float32)

    f3_ref[...] = f1_ref[...].astype(jnp.bfloat16)
    m_ref[...] = jnp.dot(f3_ref[pl.ds(wp, (rows - 2) * wp), :], g3_ref[...],
                         preferred_element_type=jnp.float32)

    def body2(q, carry):
        f2 = update(f1_ref, q)
        f2 = pltpu.roll(f2, wp - CH, 0)
        o_ref[0, q - RH] = f2[: wp - 2 * CH]
        return carry

    lax.fori_loop(RH, rows - RH, body2, 0)


def per_device(images, rates, smoothing):
    kernel, gram, lam, step = kernel_parts(rates, smoothing)
    kb = kernel.astype(jnp.bfloat16)
    g3 = (gram * step[None, :]).astype(jnp.bfloat16)
    beta = step * lam
    alpha = 1.0 - 4.0 * beta
    x = lax.all_to_all(images, "gy", split_axis=3, concat_axis=0, tiled=True)
    e, sl, h, w = x.shape
    x = halo(x, "gy", 3, CH)
    x = halo(x, "gx", 2, RH)
    hp, wp = h + 2 * RH, w + 2 * CH
    x = jnp.transpose(x, (1, 2, 3, 0)).reshape(sl, hp * wp, e)
    r = kernel.shape[1]

    gi = lax.axis_index("gx")
    gj = lax.axis_index("gy")
    grow = gi * h + jnp.arange(hp) - RH
    rm = ((grow >= 0) & (grow < h * lax.axis_size("gx"))).astype(jnp.float32)
    gcol = gj * w + jnp.arange(wp) - CH
    cv = ((gcol >= 0) & (gcol < w * lax.axis_size("gy"))).astype(jnp.float32)
    cm = jnp.broadcast_to(cv[:, None], (wp, r))

    rows = TR + 2 * RH
    nt = h // TR
    flops = 2 * sl * nt * rows * wp * r * (e + 2 * r)
    out = pl.pallas_call(
        functools.partial(fit_kernel, wp),
        out_shape=jax.ShapeDtypeStruct((sl, h, w, r), jnp.float32),
        grid=(sl, nt),
        in_specs=[
            pl.BlockSpec((1, hp * wp, e), lambda s, t: (s, 0, 0)),
            pl.BlockSpec((e, r), lambda s, t: (0, 0)),
            pl.BlockSpec((r, r), lambda s, t: (0, 0)),
            pl.BlockSpec((1, r), lambda s, t: (0, 0)),
            pl.BlockSpec((1, r), lambda s, t: (0, 0)),
            pl.BlockSpec((1, r), lambda s, t: (0, 0)),
            pl.BlockSpec((wp, r), lambda s, t: (0, 0)),
            pl.BlockSpec(memory_space=pltpu.SMEM),
        ],
        out_specs=pl.BlockSpec((1, TR, w, r), lambda s, t: (s, t, 0, 0)),
        scratch_shapes=[
            pltpu.VMEM((rows * wp, r), jnp.float32),
            pltpu.VMEM((rows * wp, r), jnp.float32),
            pltpu.VMEM((rows * wp, r), jnp.float32),
            pltpu.VMEM((rows * wp, r), jnp.bfloat16),
            pltpu.VMEM(((rows - 2) * wp, r), jnp.float32),
        ],
        compiler_params=pltpu.CompilerParams(
            dimension_semantics=("arbitrary", "arbitrary"),
            vmem_limit_bytes=48 * 1024 * 1024,
        ),
        cost_estimate=pl.CostEstimate(
            flops=flops, transcendentals=0,
            bytes_accessed=sl * (hp * wp * e * 2 + h * w * r * 4),
        ),
    )(x, kb, g3, step[None, :], alpha[None, :], beta[None, :], cm, rm)
    return out


def solution(mesh):
    in_specs = (P("gy", None, "gx", None), P(), P())
    out_specs = P(None, "gx", "gy", None)
    return jax.shard_map(
        per_device, mesh=mesh, in_specs=in_specs, out_specs=out_specs, check_vma=False
    )
```

```python
import functools

import jax
import jax.numpy as jnp
from jax import lax
from jax.experimental import pallas as pl
from jax.experimental.pallas import tpu as pltpu
from jax.sharding import PartitionSpec as P

E = 64
ITERS = 3
RH = 2
CH = 4
TR = 64


def kernel_parts(rates, smoothing):
    times = 10.0 * (jnp.arange(E, dtype=jnp.float32) + 1.0)
    raw = jnp.exp(-times[:, None] * rates[None, :])
    kernel = raw / jnp.sqrt(jnp.sum(raw * raw, axis=0))[None, :]
    gram = jnp.dot(kernel.T, kernel, precision=lax.Precision.HIGHEST)
    rowsum = jnp.sum(gram, axis=1)
    lam = smoothing * rowsum
    step = 1.0 / (rowsum + 8.0 * lam)
    return (kernel, gram, lam, step)


def halo(cells, axis, dim, width):
    count = lax.axis_size(axis)
    head = lax.slice_in_dim(cells, 0, width, axis=dim)
    tail = lax.slice_in_dim(cells, cells.shape[dim] - width, cells.shape[dim], axis=dim)
    return jnp.concatenate(
        [
            lax.ppermute(tail, axis, [(i, i + 1) for i in range(count - 1)]),
            cells,
            lax.ppermute(head, axis, [(i + 1, i) for i in range(count - 1)]),
        ],
        axis=dim,
    )


def fit_kernel(wp, x_ref, kb_ref, g3_ref, step_ref, alpha_ref, beta_ref, cm_ref, rm_ref,
               o_ref, b_ref, f0_ref, f1_ref, f3_ref, m_ref):
    t = pl.program_id(1)
    rows = TR + 2 * RH
    n = rows * wp
    base = pl.multiple_of(t * (TR * wp), 16)
    step = step_ref[...]
    alpha = alpha_ref[...]
    beta = beta_ref[...]
    cm = cm_ref[...]

    sb = jnp.dot(x_ref[0, pl.ds(base, n), :], kb_ref[...],
                 preferred_element_type=jnp.float32) * step
    b_ref[...] = sb
    f0 = jnp.maximum(sb, 0.0)
    f0_ref[...] = f0
    f3_ref[...] = f0.astype(jnp.bfloat16)

    def update(src_ref, q):
        o = pl.multiple_of(q * wp, 8)
        c = src_ref[pl.ds(o, wp), :]
        up = src_ref[pl.ds(o - wp, wp), :]
        dn = src_ref[pl.ds(o + wp, wp), :]
        lf = pltpu.roll(c, 1, 0)
        rt = pltpu.roll(c, wp - 1, 0)
        nb = (up + dn) + (lf + rt)
        v = (alpha * c + beta * nb) + (b_ref[pl.ds(o, wp), :] - m_ref[pl.ds(o - wp, wp), :])
        return jnp.maximum(v, 0.0)

    m_ref[...] = jnp.dot(f3_ref[pl.ds(wp, (rows - 2) * wp), :], g3_ref[...],
                         preferred_element_type=jnp.float32)

    def body1(q, carry):
        f1 = update(f0_ref, q) * (cm * rm_ref[t * TR + q])
        f1_ref[pl.ds(pl.multiple_of(q * wp, 8), wp), :] = f1
        return carry

    lax.fori_loop(1, rows - 1, body1, 0)
    f1_ref[pl.ds(0, wp), :] = jnp.zeros((wp, f1_ref.shape[1]), jnp.float32)
    f1_ref[pl.ds((rows - 1) * wp, wp), :] = jnp.zeros((wp, f1_ref.shape[1]), jnp.float32)

    f3_ref[...] = f1_ref[...].astype(jnp.bfloat16)
    m_ref[...] = jnp.dot(f3_ref[pl.ds(wp, (rows - 2) * wp), :], g3_ref[...],
                         preferred_element_type=jnp.float32)

    def body2(q, carry):
        f2 = update(f1_ref, q)
        f2 = pltpu.roll(f2, wp - CH, 0)
        o_ref[0, q - RH] = f2[: wp - 2 * CH]
        return carry

    lax.fori_loop(RH, rows - RH, body2, 0)


def per_device(images, rates, smoothing):
    kernel, gram, lam, step = kernel_parts(rates, smoothing)
    kb = kernel.astype(jnp.bfloat16)
    g3 = (gram * step[None, :]).astype(jnp.bfloat16)
    beta = step * lam
    alpha = 1.0 - 4.0 * beta
    x = lax.all_to_all(images, "gy", split_axis=3, concat_axis=0, tiled=True)
    e, sl, h, w = x.shape
    x = halo(x, "gy", 3, CH)
    x = halo(x, "gx", 2, RH)
    hp, wp = h + 2 * RH, w + 2 * CH
    x = jnp.transpose(x, (1, 2, 3, 0)).reshape(sl, hp * wp, e)
    r = kernel.shape[1]

    gi = lax.axis_index("gx")
    gj = lax.axis_index("gy")
    grow = gi * h + jnp.arange(hp) - RH
    rm = ((grow >= 0) & (grow < h * lax.axis_size("gx"))).astype(jnp.float32)
    gcol = gj * w + jnp.arange(wp) - CH
    cv = ((gcol >= 0) & (gcol < w * lax.axis_size("gy"))).astype(jnp.float32)
    cm = jnp.broadcast_to(cv[:, None], (wp, r))

    rows = TR + 2 * RH
    nt = h // TR
    flops = 2 * sl * nt * rows * wp * r * (e + 2 * r)
    out = pl.pallas_call(
        functools.partial(fit_kernel, wp),
        out_shape=jax.ShapeDtypeStruct((sl, h, w, r), jnp.float32),
        grid=(sl, nt),
        in_specs=[
            pl.BlockSpec((1, hp * wp, e), lambda s, t: (s, 0, 0)),
            pl.BlockSpec((e, r), lambda s, t: (0, 0)),
            pl.BlockSpec((r, r), lambda s, t: (0, 0)),
            pl.BlockSpec((1, r), lambda s, t: (0, 0)),
            pl.BlockSpec((1, r), lambda s, t: (0, 0)),
            pl.BlockSpec((1, r), lambda s, t: (0, 0)),
            pl.BlockSpec((wp, r), lambda s, t: (0, 0)),
            pl.BlockSpec(memory_space=pltpu.SMEM),
        ],
        out_specs=pl.BlockSpec((1, TR, w, r), lambda s, t: (s, t, 0, 0)),
        scratch_shapes=[
            pltpu.VMEM((rows * wp, r), jnp.float32),
            pltpu.VMEM((rows * wp, r), jnp.float32),
            pltpu.VMEM((rows * wp, r), jnp.float32),
            pltpu.VMEM((rows * wp, r), jnp.bfloat16),
            pltpu.VMEM(((rows - 2) * wp, r), jnp.float32),
        ],
        compiler_params=pltpu.CompilerParams(
            dimension_semantics=("arbitrary", "arbitrary"),
            vmem_limit_bytes=48 * 1024 * 1024,
        ),
        cost_estimate=pl.CostEstimate(
            flops=flops, transcendentals=0,
            bytes_accessed=sl * (hp * wp * e * 2 + h * w * r * 4),
        ),
    )(x, kb, g3, step[None, :], alpha[None, :], beta[None, :], cm, rm)
    return out


def solution(mesh):
    in_specs = (P("gy", None, "gx", None), P(), P())
    out_specs = P(None, "gx", "gy", None)
    return jax.shard_map(
        per_device, mesh=mesh, in_specs=in_specs, out_specs=out_specs, check_vma=False
    )
```

```python
import functools

import jax
import jax.numpy as jnp
from jax import lax
from jax.experimental import pallas as pl
from jax.experimental.pallas import tpu as pltpu
from jax.sharding import PartitionSpec as P

E = 64
ITERS = 3
RH = 2
CH = 4
TR = 64


def kernel_parts(rates, smoothing):
    times = 10.0 * (jnp.arange(E, dtype=jnp.float32) + 1.0)
    raw = jnp.exp(-times[:, None] * rates[None, :])
    kernel = raw / jnp.sqrt(jnp.sum(raw * raw, axis=0))[None, :]
    gram = jnp.dot(kernel.T, kernel, precision=lax.Precision.HIGHEST)
    rowsum = jnp.sum(gram, axis=1)
    lam = smoothing * rowsum
    step = 1.0 / (rowsum + 8.0 * lam)
    return (kernel, gram, lam, step)


def halo(cells, axis, dim, width):
    count = lax.axis_size(axis)
    head = lax.slice_in_dim(cells, 0, width, axis=dim)
    tail = lax.slice_in_dim(cells, cells.shape[dim] - width, cells.shape[dim], axis=dim)
    return jnp.concatenate(
        [
            lax.ppermute(tail, axis, [(i, i + 1) for i in range(count - 1)]),
            cells,
            lax.ppermute(head, axis, [(i + 1, i) for i in range(count - 1)]),
        ],
        axis=dim,
    )


def fit_kernel(wp, x_ref, kb_ref, g3_ref, step_ref, alpha_ref, beta_ref, cm_ref, rm_ref,
               o_ref, b_ref, f0_ref, f1_ref, f3_ref, m_ref):
    t = pl.program_id(1)
    rows = TR + 2 * RH
    n = rows * wp
    base = pl.multiple_of(t * (TR * wp), 16)
    step = step_ref[...]
    alpha = alpha_ref[...]
    beta = beta_ref[...]
    cm = cm_ref[...]

    sb = jnp.dot(x_ref[0, pl.ds(base, n), :].astype(jnp.bfloat16), kb_ref[...],
                 preferred_element_type=jnp.float32) * step
    b_ref[...] = sb
    f0 = jnp.maximum(sb, 0.0)
    f0_ref[...] = f0
    f3_ref[...] = f0.astype(jnp.bfloat16)

    def update(src_ref, q):
        o = pl.multiple_of(q * wp, 8)
        c = src_ref[pl.ds(o, wp), :]
        up = src_ref[pl.ds(o - wp, wp), :]
        dn = src_ref[pl.ds(o + wp, wp), :]
        lf = pltpu.roll(c, 1, 0)
        rt = pltpu.roll(c, wp - 1, 0)
        nb = (up + dn) + (lf + rt)
        v = (alpha * c + beta * nb) + (b_ref[pl.ds(o, wp), :] - m_ref[pl.ds(o - wp, wp), :])
        return jnp.maximum(v, 0.0)

    m_ref[...] = jnp.dot(f3_ref[pl.ds(wp, (rows - 2) * wp), :], g3_ref[...],
                         preferred_element_type=jnp.float32)

    def body1(q, carry):
        f1 = update(f0_ref, q) * (cm * rm_ref[t * TR + q])
        f1_ref[pl.ds(pl.multiple_of(q * wp, 8), wp), :] = f1
        return carry

    lax.fori_loop(1, rows - 1, body1, 0)
    f1_ref[pl.ds(0, wp), :] = jnp.zeros((wp, f1_ref.shape[1]), jnp.float32)
    f1_ref[pl.ds((rows - 1) * wp, wp), :] = jnp.zeros((wp, f1_ref.shape[1]), jnp.float32)

    f3_ref[...] = f1_ref[...].astype(jnp.bfloat16)
    m_ref[...] = jnp.dot(f3_ref[pl.ds(wp, (rows - 2) * wp), :], g3_ref[...],
                         preferred_element_type=jnp.float32)

    def body2(q, carry):
        f2 = update(f1_ref, q)
        f2 = pltpu.roll(f2, wp - CH, 0)
        o_ref[0, q - RH] = f2[: wp - 2 * CH]
        return carry

    lax.fori_loop(RH, rows - RH, body2, 0)


def per_device(images, rates, smoothing):
    kernel, gram, lam, step = kernel_parts(rates, smoothing)
    kb = kernel.astype(jnp.bfloat16)
    g3 = (gram * step[None, :]).astype(jnp.bfloat16)
    beta = step * lam
    alpha = 1.0 - 4.0 * beta
    x = lax.all_to_all(images, "gy", split_axis=3, concat_axis=0, tiled=True)
    e, sl, h, w = x.shape
    x = halo(x, "gy", 3, CH)
    x = halo(x, "gx", 2, RH)
    hp, wp = h + 2 * RH, w + 2 * CH
    eye = jnp.eye(e, dtype=jnp.bfloat16)
    x = jnp.einsum("esij,ef->sijf", x, eye, preferred_element_type=jnp.float32)
    x = x.reshape(sl, hp * wp, e)
    r = kernel.shape[1]

    gi = lax.axis_index("gx")
    gj = lax.axis_index("gy")
    grow = gi * h + jnp.arange(hp) - RH
    rm = ((grow >= 0) & (grow < h * lax.axis_size("gx"))).astype(jnp.float32)
    gcol = gj * w + jnp.arange(wp) - CH
    cv = ((gcol >= 0) & (gcol < w * lax.axis_size("gy"))).astype(jnp.float32)
    cm = jnp.broadcast_to(cv[:, None], (wp, r))

    rows = TR + 2 * RH
    nt = h // TR
    flops = 2 * sl * nt * rows * wp * r * (e + 2 * r)
    out = pl.pallas_call(
        functools.partial(fit_kernel, wp),
        out_shape=jax.ShapeDtypeStruct((sl, h, w, r), jnp.float32),
        grid=(sl, nt),
        in_specs=[
            pl.BlockSpec((1, hp * wp, e), lambda s, t: (s, 0, 0)),
            pl.BlockSpec((e, r), lambda s, t: (0, 0)),
            pl.BlockSpec((r, r), lambda s, t: (0, 0)),
            pl.BlockSpec((1, r), lambda s, t: (0, 0)),
            pl.BlockSpec((1, r), lambda s, t: (0, 0)),
            pl.BlockSpec((1, r), lambda s, t: (0, 0)),
            pl.BlockSpec((wp, r), lambda s, t: (0, 0)),
            pl.BlockSpec(memory_space=pltpu.SMEM),
        ],
        out_specs=pl.BlockSpec((1, TR, w, r), lambda s, t: (s, t, 0, 0)),
        scratch_shapes=[
            pltpu.VMEM((rows * wp, r), jnp.float32),
            pltpu.VMEM((rows * wp, r), jnp.float32),
            pltpu.VMEM((rows * wp, r), jnp.float32),
            pltpu.VMEM((rows * wp, r), jnp.bfloat16),
            pltpu.VMEM(((rows - 2) * wp, r), jnp.float32),
        ],
        compiler_params=pltpu.CompilerParams(
            dimension_semantics=("arbitrary", "arbitrary"),
            vmem_limit_bytes=48 * 1024 * 1024,
        ),
        cost_estimate=pl.CostEstimate(
            flops=flops, transcendentals=0,
            bytes_accessed=sl * (hp * wp * e * 4 + h * w * r * 4),
        ),
    )(x, kb, g3, step[None, :], alpha[None, :], beta[None, :], cm, rm)
    return out


def solution(mesh):
    in_specs = (P("gy", None, "gx", None), P(), P())
    out_specs = P(None, "gx", "gy", None)
    return jax.shard_map(
        per_device, mesh=mesh, in_specs=in_specs, out_specs=out_specs, check_vma=False
    )
```

```python
import functools

import jax
import jax.numpy as jnp
from jax import lax
from jax.experimental import pallas as pl
from jax.experimental.pallas import tpu as pltpu
from jax.experimental.layout import Layout, with_layout_constraint
from jax.sharding import PartitionSpec as P

E = 64
ITERS = 3
RH = 2
CH = 4
TR = 64


def kernel_parts(rates, smoothing):
    times = 10.0 * (jnp.arange(E, dtype=jnp.float32) + 1.0)
    raw = jnp.exp(-times[:, None] * rates[None, :])
    kernel = raw / jnp.sqrt(jnp.sum(raw * raw, axis=0))[None, :]
    gram = jnp.dot(kernel.T, kernel, precision=lax.Precision.HIGHEST)
    rowsum = jnp.sum(gram, axis=1)
    lam = smoothing * rowsum
    step = 1.0 / (rowsum + 8.0 * lam)
    return (kernel, gram, lam, step)


def halo(cells, axis, dim, width):
    count = lax.axis_size(axis)
    head = lax.slice_in_dim(cells, 0, width, axis=dim)
    tail = lax.slice_in_dim(cells, cells.shape[dim] - width, cells.shape[dim], axis=dim)
    return jnp.concatenate(
        [
            lax.ppermute(tail, axis, [(i, i + 1) for i in range(count - 1)]),
            cells,
            lax.ppermute(head, axis, [(i + 1, i) for i in range(count - 1)]),
        ],
        axis=dim,
    )


def fit_kernel(wp, x_ref, kb_ref, g3_ref, step_ref, alpha_ref, beta_ref, cm_ref, rm_ref,
               o_ref, b_ref, f0_ref, f1_ref, f3_ref, m_ref):
    t = pl.program_id(1)
    rows = TR + 2 * RH
    n = rows * wp
    base = pl.multiple_of(t * (TR * wp), 16)
    step = step_ref[...]
    alpha = alpha_ref[...]
    beta = beta_ref[...]
    cm = cm_ref[...]

    sb = jnp.dot(x_ref[0, pl.ds(base, n), :].astype(jnp.bfloat16), kb_ref[...],
                 preferred_element_type=jnp.float32) * step
    b_ref[...] = sb
    f0 = jnp.maximum(sb, 0.0)
    f0_ref[...] = f0
    f3_ref[...] = f0.astype(jnp.bfloat16)

    def update(src_ref, q):
        o = pl.multiple_of(q * wp, 8)
        c = src_ref[pl.ds(o, wp), :]
        up = src_ref[pl.ds(o - wp, wp), :]
        dn = src_ref[pl.ds(o + wp, wp), :]
        lf = pltpu.roll(c, 1, 0)
        rt = pltpu.roll(c, wp - 1, 0)
        nb = (up + dn) + (lf + rt)
        v = (alpha * c + beta * nb) + (b_ref[pl.ds(o, wp), :] - m_ref[pl.ds(o - wp, wp), :])
        return jnp.maximum(v, 0.0)

    m_ref[...] = jnp.dot(f3_ref[pl.ds(wp, (rows - 2) * wp), :], g3_ref[...],
                         preferred_element_type=jnp.float32)

    def body1(q, carry):
        f1 = update(f0_ref, q) * (cm * rm_ref[t * TR + q])
        f1_ref[pl.ds(pl.multiple_of(q * wp, 8), wp), :] = f1
        return carry

    lax.fori_loop(1, rows - 1, body1, 0)
    f1_ref[pl.ds(0, wp), :] = jnp.zeros((wp, f1_ref.shape[1]), jnp.float32)
    f1_ref[pl.ds((rows - 1) * wp, wp), :] = jnp.zeros((wp, f1_ref.shape[1]), jnp.float32)

    f3_ref[...] = f1_ref[...].astype(jnp.bfloat16)
    m_ref[...] = jnp.dot(f3_ref[pl.ds(wp, (rows - 2) * wp), :], g3_ref[...],
                         preferred_element_type=jnp.float32)

    def body2(q, carry):
        f2 = update(f1_ref, q)
        f2 = pltpu.roll(f2, wp - CH, 0)
        o_ref[0, q - RH] = f2[: wp - 2 * CH]
        return carry

    lax.fori_loop(RH, rows - RH, body2, 0)


def pin(x):
    return with_layout_constraint(x, Layout(tuple(range(x.ndim))))


def per_device(images, rates, smoothing):
    kernel, gram, lam, step = kernel_parts(rates, smoothing)
    kb = kernel.astype(jnp.bfloat16)
    g3 = (gram * step[None, :]).astype(jnp.bfloat16)
    beta = step * lam
    alpha = 1.0 - 4.0 * beta
    x = lax.all_to_all(images, "gy", split_axis=3, concat_axis=0, tiled=True)
    e, sl, h, w = x.shape
    hp, wp = h + 2 * RH, w + 2 * CH
    eye = jnp.eye(e, dtype=jnp.bfloat16)
    x = jnp.einsum("esij,ef->sijf", x, eye, preferred_element_type=jnp.float32)
    x = pin(x)
    x = pin(halo(x, "gy", 2, CH))
    x = pin(halo(x, "gx", 1, RH))
    x = x.reshape(sl, hp * wp, e)
    r = kernel.shape[1]

    gi = lax.axis_index("gx")
    gj = lax.axis_index("gy")
    grow = gi * h + jnp.arange(hp) - RH
    rm = ((grow >= 0) & (grow < h * lax.axis_size("gx"))).astype(jnp.float32)
    gcol = gj * w + jnp.arange(wp) - CH
    cv = ((gcol >= 0) & (gcol < w * lax.axis_size("gy"))).astype(jnp.float32)
    cm = jnp.broadcast_to(cv[:, None], (wp, r))

    rows = TR + 2 * RH
    nt = h // TR
    flops = 2 * sl * nt * rows * wp * r * (e + 2 * r)
    out = pl.pallas_call(
        functools.partial(fit_kernel, wp),
        out_shape=jax.ShapeDtypeStruct((sl, h, w, r), jnp.float32),
        grid=(sl, nt),
        in_specs=[
            pl.BlockSpec((1, hp * wp, e), lambda s, t: (s, 0, 0)),
            pl.BlockSpec((e, r), lambda s, t: (0, 0)),
            pl.BlockSpec((r, r), lambda s, t: (0, 0)),
            pl.BlockSpec((1, r), lambda s, t: (0, 0)),
            pl.BlockSpec((1, r), lambda s, t: (0, 0)),
            pl.BlockSpec((1, r), lambda s, t: (0, 0)),
            pl.BlockSpec((wp, r), lambda s, t: (0, 0)),
            pl.BlockSpec(memory_space=pltpu.SMEM),
        ],
        out_specs=pl.BlockSpec((1, TR, w, r), lambda s, t: (s, t, 0, 0)),
        scratch_shapes=[
            pltpu.VMEM((rows * wp, r), jnp.float32),
            pltpu.VMEM((rows * wp, r), jnp.float32),
            pltpu.VMEM((rows * wp, r), jnp.float32),
            pltpu.VMEM((rows * wp, r), jnp.bfloat16),
            pltpu.VMEM(((rows - 2) * wp, r), jnp.float32),
        ],
        compiler_params=pltpu.CompilerParams(
            dimension_semantics=("arbitrary", "arbitrary"),
            vmem_limit_bytes=48 * 1024 * 1024,
        ),
        cost_estimate=pl.CostEstimate(
            flops=flops, transcendentals=0,
            bytes_accessed=sl * (hp * wp * e * 4 + h * w * r * 4),
        ),
    )(x, kb, g3, step[None, :], alpha[None, :], beta[None, :], cm, rm)
    return out


def solution(mesh):
    in_specs = (P("gy", None, "gx", None), P(), P())
    out_specs = P(None, "gx", "gy", None)
    return jax.shard_map(
        per_device, mesh=mesh, in_specs=in_specs, out_specs=out_specs, check_vma=False
    )
```

```python
import functools

import jax
import jax.numpy as jnp
from jax import lax
from jax.experimental import pallas as pl
from jax.experimental.pallas import tpu as pltpu
from jax.experimental.layout import Layout, with_layout_constraint
from jax.sharding import PartitionSpec as P

E = 64
ITERS = 3
RH = 2
CH = 4
TR = 64


def kernel_parts(rates, smoothing):
    times = 10.0 * (jnp.arange(E, dtype=jnp.float32) + 1.0)
    raw = jnp.exp(-times[:, None] * rates[None, :])
    kernel = raw / jnp.sqrt(jnp.sum(raw * raw, axis=0))[None, :]
    gram = jnp.dot(kernel.T, kernel, precision=lax.Precision.HIGHEST)
    rowsum = jnp.sum(gram, axis=1)
    lam = smoothing * rowsum
    step = 1.0 / (rowsum + 8.0 * lam)
    return (kernel, gram, lam, step)


def halo(cells, axis, dim, width):
    count = lax.axis_size(axis)
    head = lax.slice_in_dim(cells, 0, width, axis=dim)
    tail = lax.slice_in_dim(cells, cells.shape[dim] - width, cells.shape[dim], axis=dim)
    return jnp.concatenate(
        [
            lax.ppermute(tail, axis, [(i, i + 1) for i in range(count - 1)]),
            cells,
            lax.ppermute(head, axis, [(i + 1, i) for i in range(count - 1)]),
        ],
        axis=dim,
    )


def fit_kernel(wp, x_ref, kb_ref, g3_ref, step_ref, alpha_ref, beta_ref, cm_ref, rm_ref,
               o_ref, b_ref, f0_ref, f1_ref, f3_ref, m_ref):
    t = pl.program_id(1)
    rows = TR + 2 * RH
    n = rows * wp
    base = pl.multiple_of(t * (TR * wp), 16)
    step = step_ref[...]
    alpha = alpha_ref[...]
    beta = beta_ref[...]
    cm = cm_ref[...]

    xt = x_ref[0, pl.ds(t * TR, rows)].astype(jnp.float32).reshape(n, x_ref.shape[3])
    sb = jnp.dot(xt.astype(jnp.bfloat16), kb_ref[...],
                 preferred_element_type=jnp.float32) * step
    b_ref[...] = sb
    f0 = jnp.maximum(sb, 0.0)
    f0_ref[...] = f0
    f3_ref[...] = f0.astype(jnp.bfloat16)

    def update(src_ref, q):
        o = pl.multiple_of(q * wp, 8)
        c = src_ref[pl.ds(o, wp), :]
        up = src_ref[pl.ds(o - wp, wp), :]
        dn = src_ref[pl.ds(o + wp, wp), :]
        lf = pltpu.roll(c, 1, 0)
        rt = pltpu.roll(c, wp - 1, 0)
        nb = (up + dn) + (lf + rt)
        v = (alpha * c + beta * nb) + (b_ref[pl.ds(o, wp), :] - m_ref[pl.ds(o - wp, wp), :])
        return jnp.maximum(v, 0.0)

    m_ref[...] = jnp.dot(f3_ref[pl.ds(wp, (rows - 2) * wp), :], g3_ref[...],
                         preferred_element_type=jnp.float32)

    def body1(q, carry):
        f1 = update(f0_ref, q) * (cm * rm_ref[t * TR + q])
        f1_ref[pl.ds(pl.multiple_of(q * wp, 8), wp), :] = f1
        return carry

    lax.fori_loop(1, rows - 1, body1, 0)
    f1_ref[pl.ds(0, wp), :] = jnp.zeros((wp, f1_ref.shape[1]), jnp.float32)
    f1_ref[pl.ds((rows - 1) * wp, wp), :] = jnp.zeros((wp, f1_ref.shape[1]), jnp.float32)

    f3_ref[...] = f1_ref[...].astype(jnp.bfloat16)
    m_ref[...] = jnp.dot(f3_ref[pl.ds(wp, (rows - 2) * wp), :], g3_ref[...],
                         preferred_element_type=jnp.float32)

    def body2(q, carry):
        f2 = update(f1_ref, q)
        f2 = pltpu.roll(f2, wp - CH, 0)
        o_ref[0, q - RH] = f2[: wp - 2 * CH]
        return carry

    lax.fori_loop(RH, rows - RH, body2, 0)


def pin(x):
    return with_layout_constraint(x, Layout(tuple(range(x.ndim))))


def per_device(images, rates, smoothing):
    kernel, gram, lam, step = kernel_parts(rates, smoothing)
    kb = kernel.astype(jnp.bfloat16)
    g3 = (gram * step[None, :]).astype(jnp.bfloat16)
    beta = step * lam
    alpha = 1.0 - 4.0 * beta
    x = lax.all_to_all(images, "gy", split_axis=3, concat_axis=0, tiled=True)
    e, sl, h, w = x.shape
    hp, wp = h + 2 * RH, w + 2 * CH
    x = pin(jnp.transpose(x, (1, 2, 3, 0)))
    x = pin(halo(x, "gy", 2, CH))
    x = pin(halo(x, "gx", 1, RH))
    r = kernel.shape[1]

    gi = lax.axis_index("gx")
    gj = lax.axis_index("gy")
    grow = gi * h + jnp.arange(hp) - RH
    rm = ((grow >= 0) & (grow < h * lax.axis_size("gx"))).astype(jnp.float32)
    gcol = gj * w + jnp.arange(wp) - CH
    cv = ((gcol >= 0) & (gcol < w * lax.axis_size("gy"))).astype(jnp.float32)
    cm = jnp.broadcast_to(cv[:, None], (wp, r))

    rows = TR + 2 * RH
    nt = h // TR
    flops = 2 * sl * nt * rows * wp * r * (e + 2 * r)
    out = pl.pallas_call(
        functools.partial(fit_kernel, wp),
        out_shape=jax.ShapeDtypeStruct((sl, h, w, r), jnp.float32),
        grid=(sl, nt),
        in_specs=[
            pl.BlockSpec((1, hp, wp, e), lambda s, t: (s, 0, 0, 0)),
            pl.BlockSpec((e, r), lambda s, t: (0, 0)),
            pl.BlockSpec((r, r), lambda s, t: (0, 0)),
            pl.BlockSpec((1, r), lambda s, t: (0, 0)),
            pl.BlockSpec((1, r), lambda s, t: (0, 0)),
            pl.BlockSpec((1, r), lambda s, t: (0, 0)),
            pl.BlockSpec((wp, r), lambda s, t: (0, 0)),
            pl.BlockSpec(memory_space=pltpu.SMEM),
        ],
        out_specs=pl.BlockSpec((1, TR, w, r), lambda s, t: (s, t, 0, 0)),
        scratch_shapes=[
            pltpu.VMEM((rows * wp, r), jnp.float32),
            pltpu.VMEM((rows * wp, r), jnp.float32),
            pltpu.VMEM((rows * wp, r), jnp.float32),
            pltpu.VMEM((rows * wp, r), jnp.bfloat16),
            pltpu.VMEM(((rows - 2) * wp, r), jnp.float32),
        ],
        compiler_params=pltpu.CompilerParams(
            dimension_semantics=("arbitrary", "arbitrary"),
            vmem_limit_bytes=48 * 1024 * 1024,
        ),
        cost_estimate=pl.CostEstimate(
            flops=flops, transcendentals=0,
            bytes_accessed=sl * (hp * wp * e * 2 + h * w * r * 4),
        ),
    )(x, kb, g3, step[None, :], alpha[None, :], beta[None, :], cm, rm)
    return out


def solution(mesh):
    in_specs = (P("gy", None, "gx", None), P(), P())
    out_specs = P(None, "gx", "gy", None)
    return jax.shard_map(
        per_device, mesh=mesh, in_specs=in_specs, out_specs=out_specs, check_vma=False
    )
```

```python
import functools

import jax
import jax.numpy as jnp
from jax import lax
from jax.experimental import pallas as pl
from jax.experimental.pallas import tpu as pltpu
from jax.experimental.layout import Layout, with_layout_constraint
from jax.sharding import PartitionSpec as P

E = 64
ITERS = 3
RH = 2
CH = 4
TR = 64


def kernel_parts(rates, smoothing):
    times = 10.0 * (jnp.arange(E, dtype=jnp.float32) + 1.0)
    raw = jnp.exp(-times[:, None] * rates[None, :])
    kernel = raw / jnp.sqrt(jnp.sum(raw * raw, axis=0))[None, :]
    gram = jnp.dot(kernel.T, kernel, precision=lax.Precision.HIGHEST)
    rowsum = jnp.sum(gram, axis=1)
    lam = smoothing * rowsum
    step = 1.0 / (rowsum + 8.0 * lam)
    return (kernel, gram, lam, step)


def halo(cells, axis, dim, width):
    count = lax.axis_size(axis)
    head = lax.slice_in_dim(cells, 0, width, axis=dim)
    tail = lax.slice_in_dim(cells, cells.shape[dim] - width, cells.shape[dim], axis=dim)
    return jnp.concatenate(
        [
            lax.ppermute(tail, axis, [(i, i + 1) for i in range(count - 1)]),
            cells,
            lax.ppermute(head, axis, [(i + 1, i) for i in range(count - 1)]),
        ],
        axis=dim,
    )


def fit_kernel(wp, x_ref, kb_ref, g3_ref, step_ref, alpha_ref, beta_ref, cm_ref, rm_ref,
               o_ref, b_ref, f0_ref, f1_ref, f3_ref, m_ref):
    t = pl.program_id(1)
    rows = TR + 2 * RH
    n = rows * wp
    base = pl.multiple_of(t * (TR * wp), 16)
    step = step_ref[...]
    alpha = alpha_ref[...]
    beta = beta_ref[...]
    cm = cm_ref[...]

    xt = x_ref[0, pl.ds(t * TR, rows)].astype(jnp.float32).reshape(n, x_ref.shape[3])
    sb = jnp.dot(xt.astype(jnp.bfloat16), kb_ref[...],
                 preferred_element_type=jnp.float32) * step
    b_ref[...] = sb
    f0 = jnp.maximum(sb, 0.0)
    f0_ref[...] = f0
    f3_ref[...] = f0.astype(jnp.bfloat16)

    def update(src_ref, q):
        o = pl.multiple_of(q * wp, 8)
        c = src_ref[pl.ds(o, wp), :]
        up = src_ref[pl.ds(o - wp, wp), :]
        dn = src_ref[pl.ds(o + wp, wp), :]
        lf = pltpu.roll(c, 1, 0)
        rt = pltpu.roll(c, wp - 1, 0)
        nb = (up + dn) + (lf + rt)
        v = (alpha * c + beta * nb) + (b_ref[pl.ds(o, wp), :] - m_ref[pl.ds(o - wp, wp), :])
        return jnp.maximum(v, 0.0)

    m_ref[...] = jnp.dot(f3_ref[pl.ds(wp, (rows - 2) * wp), :], g3_ref[...],
                         preferred_element_type=jnp.float32)

    def body1(q, carry):
        f1 = update(f0_ref, q) * (cm * rm_ref[t * TR + q])
        f1_ref[pl.ds(pl.multiple_of(q * wp, 8), wp), :] = f1
        return carry

    lax.fori_loop(1, rows - 1, body1, 0)
    f1_ref[pl.ds(0, wp), :] = jnp.zeros((wp, f1_ref.shape[1]), jnp.float32)
    f1_ref[pl.ds((rows - 1) * wp, wp), :] = jnp.zeros((wp, f1_ref.shape[1]), jnp.float32)

    f3_ref[...] = f1_ref[...].astype(jnp.bfloat16)
    m_ref[...] = jnp.dot(f3_ref[pl.ds(wp, (rows - 2) * wp), :], g3_ref[...],
                         preferred_element_type=jnp.float32)

    def body2(q, carry):
        f2 = update(f1_ref, q)
        f2 = pltpu.roll(f2, wp - CH, 0)
        o_ref[0, q - RH] = f2[: wp - 2 * CH]
        return carry

    lax.fori_loop(RH, rows - RH, body2, 0)


def halo2d(x, rh, ch):
    nx, ny = lax.axis_size("gx"), lax.axis_size("gy")
    h, w = x.shape[1], x.shape[2]
    rows = {-1: (h - rh, h), 0: (0, h), 1: (0, rh)}
    cols = {-1: (w - ch, w), 0: (0, w), 1: (0, ch)}

    def piece(di, dj):
        p = x[:, rows[di][0]:rows[di][1], cols[dj][0]:cols[dj][1]]
        if di == 0 and dj == 0:
            return p
        pairs = []
        for i in range(nx):
            for j in range(ny):
                si, sj = i + di, j + dj
                if 0 <= si < nx and 0 <= sj < ny:
                    pairs.append((si * ny + sj, i * ny + j))
        return lax.ppermute(p, ("gx", "gy"), pairs)

    band = [jnp.concatenate([piece(di, -1), piece(di, 0), piece(di, 1)], axis=2)
            for di in (-1, 0, 1)]
    return jnp.concatenate(band, axis=1)


def pin(x):
    return with_layout_constraint(x, Layout(tuple(range(x.ndim))))


def per_device(images, rates, smoothing):
    kernel, gram, lam, step = kernel_parts(rates, smoothing)
    kb = kernel.astype(jnp.bfloat16)
    g3 = (gram * step[None, :]).astype(jnp.bfloat16)
    beta = step * lam
    alpha = 1.0 - 4.0 * beta
    x = lax.all_to_all(images, "gy", split_axis=3, concat_axis=0, tiled=True)
    e, sl, h, w = x.shape
    hp, wp = h + 2 * RH, w + 2 * CH
    x = pin(jnp.transpose(x, (1, 2, 3, 0)))
    x = pin(halo2d(x, RH, CH))
    r = kernel.shape[1]

    gi = lax.axis_index("gx")
    gj = lax.axis_index("gy")
    grow = gi * h + jnp.arange(hp) - RH
    rm = ((grow >= 0) & (grow < h * lax.axis_size("gx"))).astype(jnp.float32)
    gcol = gj * w + jnp.arange(wp) - CH
    cv = ((gcol >= 0) & (gcol < w * lax.axis_size("gy"))).astype(jnp.float32)
    cm = jnp.broadcast_to(cv[:, None], (wp, r))

    rows = TR + 2 * RH
    nt = h // TR
    flops = 2 * sl * nt * rows * wp * r * (e + 2 * r)
    out = pl.pallas_call(
        functools.partial(fit_kernel, wp),
        out_shape=jax.ShapeDtypeStruct((sl, h, w, r), jnp.float32),
        grid=(sl, nt),
        in_specs=[
            pl.BlockSpec((1, hp, wp, e), lambda s, t: (s, 0, 0, 0)),
            pl.BlockSpec((e, r), lambda s, t: (0, 0)),
            pl.BlockSpec((r, r), lambda s, t: (0, 0)),
            pl.BlockSpec((1, r), lambda s, t: (0, 0)),
            pl.BlockSpec((1, r), lambda s, t: (0, 0)),
            pl.BlockSpec((1, r), lambda s, t: (0, 0)),
            pl.BlockSpec((wp, r), lambda s, t: (0, 0)),
            pl.BlockSpec(memory_space=pltpu.SMEM),
        ],
        out_specs=pl.BlockSpec((1, TR, w, r), lambda s, t: (s, t, 0, 0)),
        scratch_shapes=[
            pltpu.VMEM((rows * wp, r), jnp.float32),
            pltpu.VMEM((rows * wp, r), jnp.float32),
            pltpu.VMEM((rows * wp, r), jnp.float32),
            pltpu.VMEM((rows * wp, r), jnp.bfloat16),
            pltpu.VMEM(((rows - 2) * wp, r), jnp.float32),
        ],
        compiler_params=pltpu.CompilerParams(
            dimension_semantics=("arbitrary", "arbitrary"),
            vmem_limit_bytes=48 * 1024 * 1024,
        ),
        cost_estimate=pl.CostEstimate(
            flops=flops, transcendentals=0,
            bytes_accessed=sl * (hp * wp * e * 2 + h * w * r * 4),
        ),
    )(x, kb, g3, step[None, :], alpha[None, :], beta[None, :], cm, rm)
    return out


def solution(mesh):
    in_specs = (P("gy", None, "gx", None), P(), P())
    out_specs = P(None, "gx", "gy", None)
    return jax.shard_map(
        per_device, mesh=mesh, in_specs=in_specs, out_specs=out_specs, check_vma=False
    )
```

```python
import functools

import jax
import jax.numpy as jnp
from jax import lax
from jax.experimental import pallas as pl
from jax.experimental.pallas import tpu as pltpu
from jax.experimental.layout import Layout, with_layout_constraint
from jax.sharding import PartitionSpec as P

E = 64
ITERS = 3
RH = 2
CH = 4
TR = 64


def kernel_parts(rates, smoothing):
    times = 10.0 * (jnp.arange(E, dtype=jnp.float32) + 1.0)
    raw = jnp.exp(-times[:, None] * rates[None, :])
    kernel = raw / jnp.sqrt(jnp.sum(raw * raw, axis=0))[None, :]
    gram = jnp.dot(kernel.T, kernel, precision=lax.Precision.HIGHEST)
    rowsum = jnp.sum(gram, axis=1)
    lam = smoothing * rowsum
    step = 1.0 / (rowsum + 8.0 * lam)
    return (kernel, gram, lam, step)


def halo(cells, axis, dim, width):
    count = lax.axis_size(axis)
    head = lax.slice_in_dim(cells, 0, width, axis=dim)
    tail = lax.slice_in_dim(cells, cells.shape[dim] - width, cells.shape[dim], axis=dim)
    return jnp.concatenate(
        [
            lax.ppermute(tail, axis, [(i, i + 1) for i in range(count - 1)]),
            cells,
            lax.ppermute(head, axis, [(i + 1, i) for i in range(count - 1)]),
        ],
        axis=dim,
    )


def fit_kernel(wp, x_ref, kb_ref, g3_ref, step_ref, alpha_ref, beta_ref, cm_ref, rm_ref,
               o_ref, b_ref, f0_ref, f1_ref, f3_ref, m_ref):
    t = pl.program_id(1)
    rows = TR + 2 * RH
    n = rows * wp
    base = pl.multiple_of(t * (TR * wp), 16)
    step = step_ref[...]
    alpha = alpha_ref[...]
    beta = beta_ref[...]
    cm = cm_ref[...]

    xt = x_ref[0, pl.ds(t * TR, rows)].astype(jnp.float32).reshape(n, x_ref.shape[3])
    sb = jnp.dot(xt.astype(jnp.bfloat16), kb_ref[...],
                 preferred_element_type=jnp.float32) * step
    b_ref[...] = sb
    f0 = jnp.maximum(sb, 0.0)
    f0_ref[...] = f0
    f3_ref[...] = f0.astype(jnp.bfloat16)

    def update(src_ref, q):
        o = pl.multiple_of(q * wp, 8)
        c = src_ref[pl.ds(o, wp), :]
        up = src_ref[pl.ds(o - wp, wp), :]
        dn = src_ref[pl.ds(o + wp, wp), :]
        lf = pltpu.roll(c, 1, 0)
        rt = pltpu.roll(c, wp - 1, 0)
        nb = (up + dn) + (lf + rt)
        v = (alpha * c + beta * nb) + (b_ref[pl.ds(o, wp), :] - m_ref[pl.ds(o - wp, wp), :])
        return jnp.maximum(v, 0.0)

    m_ref[...] = jnp.dot(f3_ref[pl.ds(wp, (rows - 2) * wp), :], g3_ref[...],
                         preferred_element_type=jnp.float32)

    def body1(q, carry):
        f1 = update(f0_ref, q) * (cm * rm_ref[t * TR + q])
        f1_ref[pl.ds(pl.multiple_of(q * wp, 8), wp), :] = f1
        return carry

    lax.fori_loop(1, rows - 1, body1, 0, unroll=2)
    f1_ref[pl.ds(0, wp), :] = jnp.zeros((wp, f1_ref.shape[1]), jnp.float32)
    f1_ref[pl.ds((rows - 1) * wp, wp), :] = jnp.zeros((wp, f1_ref.shape[1]), jnp.float32)

    f3_ref[...] = f1_ref[...].astype(jnp.bfloat16)
    m_ref[...] = jnp.dot(f3_ref[pl.ds(wp, (rows - 2) * wp), :], g3_ref[...],
                         preferred_element_type=jnp.float32)

    def body2(q, carry):
        f2 = update(f1_ref, q)
        f2 = pltpu.roll(f2, wp - CH, 0)
        o_ref[0, q - RH] = f2[: wp - 2 * CH]
        return carry

    lax.fori_loop(RH, rows - RH, body2, 0, unroll=2)


def pin(x):
    return with_layout_constraint(x, Layout(tuple(range(x.ndim))))


def per_device(images, rates, smoothing):
    kernel, gram, lam, step = kernel_parts(rates, smoothing)
    kb = kernel.astype(jnp.bfloat16)
    g3 = (gram * step[None, :]).astype(jnp.bfloat16)
    beta = step * lam
    alpha = 1.0 - 4.0 * beta
    x = lax.all_to_all(images, "gy", split_axis=3, concat_axis=0, tiled=True)
    e, sl, h, w = x.shape
    hp, wp = h + 2 * RH, w + 2 * CH
    x = pin(jnp.transpose(x, (1, 2, 3, 0)))
    x = pin(halo(x, "gy", 2, CH))
    x = pin(halo(x, "gx", 1, RH))
    r = kernel.shape[1]

    gi = lax.axis_index("gx")
    gj = lax.axis_index("gy")
    grow = gi * h + jnp.arange(hp) - RH
    rm = ((grow >= 0) & (grow < h * lax.axis_size("gx"))).astype(jnp.float32)
    gcol = gj * w + jnp.arange(wp) - CH
    cv = ((gcol >= 0) & (gcol < w * lax.axis_size("gy"))).astype(jnp.float32)
    cm = jnp.broadcast_to(cv[:, None], (wp, r))

    rows = TR + 2 * RH
    nt = h // TR
    flops = 2 * sl * nt * rows * wp * r * (e + 2 * r)
    out = pl.pallas_call(
        functools.partial(fit_kernel, wp),
        out_shape=jax.ShapeDtypeStruct((sl, h, w, r), jnp.float32),
        grid=(sl, nt),
        in_specs=[
            pl.BlockSpec((1, hp, wp, e), lambda s, t: (s, 0, 0, 0)),
            pl.BlockSpec((e, r), lambda s, t: (0, 0)),
            pl.BlockSpec((r, r), lambda s, t: (0, 0)),
            pl.BlockSpec((1, r), lambda s, t: (0, 0)),
            pl.BlockSpec((1, r), lambda s, t: (0, 0)),
            pl.BlockSpec((1, r), lambda s, t: (0, 0)),
            pl.BlockSpec((wp, r), lambda s, t: (0, 0)),
            pl.BlockSpec(memory_space=pltpu.SMEM),
        ],
        out_specs=pl.BlockSpec((1, TR, w, r), lambda s, t: (s, t, 0, 0)),
        scratch_shapes=[
            pltpu.VMEM((rows * wp, r), jnp.float32),
            pltpu.VMEM((rows * wp, r), jnp.float32),
            pltpu.VMEM((rows * wp, r), jnp.float32),
            pltpu.VMEM((rows * wp, r), jnp.bfloat16),
            pltpu.VMEM(((rows - 2) * wp, r), jnp.float32),
        ],
        compiler_params=pltpu.CompilerParams(
            dimension_semantics=("arbitrary", "arbitrary"),
            vmem_limit_bytes=48 * 1024 * 1024,
        ),
        cost_estimate=pl.CostEstimate(
            flops=flops, transcendentals=0,
            bytes_accessed=sl * (hp * wp * e * 2 + h * w * r * 4),
        ),
    )(x, kb, g3, step[None, :], alpha[None, :], beta[None, :], cm, rm)
    return out


def solution(mesh):
    in_specs = (P("gy", None, "gx", None), P(), P())
    out_specs = P(None, "gx", "gy", None)
    return jax.shard_map(
        per_device, mesh=mesh, in_specs=in_specs, out_specs=out_specs, check_vma=False
    )
```

```python
import functools

import jax
import jax.numpy as jnp
from jax import lax
from jax.experimental import pallas as pl
from jax.experimental.pallas import tpu as pltpu
from jax.experimental.layout import Layout, with_layout_constraint
from jax.sharding import PartitionSpec as P

E = 64
ITERS = 3
RH = 2
CH = 4
TR = 64


def kernel_parts(rates, smoothing):
    times = 10.0 * (jnp.arange(E, dtype=jnp.float32) + 1.0)
    raw = jnp.exp(-times[:, None] * rates[None, :])
    kernel = raw / jnp.sqrt(jnp.sum(raw * raw, axis=0))[None, :]
    gram = jnp.dot(kernel.T, kernel, precision=lax.Precision.HIGHEST)
    rowsum = jnp.sum(gram, axis=1)
    lam = smoothing * rowsum
    step = 1.0 / (rowsum + 8.0 * lam)
    return (kernel, gram, lam, step)


def halo(cells, axis, dim, width):
    count = lax.axis_size(axis)
    head = lax.slice_in_dim(cells, 0, width, axis=dim)
    tail = lax.slice_in_dim(cells, cells.shape[dim] - width, cells.shape[dim], axis=dim)
    return jnp.concatenate(
        [
            lax.ppermute(tail, axis, [(i, i + 1) for i in range(count - 1)]),
            cells,
            lax.ppermute(head, axis, [(i + 1, i) for i in range(count - 1)]),
        ],
        axis=dim,
    )


def fit_kernel(wp, x_ref, kb_ref, g3_ref, step_ref, alpha_ref, beta_ref, cm_ref, rm_ref,
               o_ref, b_ref, f0_ref, f1_ref, f3_ref, m_ref):
    t = pl.program_id(1)
    rows = TR + 2 * RH
    n = rows * wp
    base = pl.multiple_of(t * (TR * wp), 16)
    step = step_ref[...]
    alpha = alpha_ref[...]
    beta = beta_ref[...]
    cm = cm_ref[...]

    xt = x_ref[0, pl.ds(t * TR, rows)].astype(jnp.float32).reshape(n, x_ref.shape[3])
    sb = jnp.dot(xt.astype(jnp.bfloat16), kb_ref[...],
                 preferred_element_type=jnp.float32) * step
    b_ref[...] = sb
    f0 = jnp.maximum(sb, 0.0)
    f0_ref[...] = f0
    inner = (rows - 2) * wp
    f3_ref[pl.ds(2 * wp, inner), :] = f0[wp:(rows - 1) * wp].astype(jnp.bfloat16)

    def update(src_ref, q):
        o = pl.multiple_of(q * wp, 8)
        c = src_ref[pl.ds(o, wp), :]
        up = src_ref[pl.ds(o - wp, wp), :]
        dn = src_ref[pl.ds(o + wp, wp), :]
        lf = pltpu.roll(c, 1, 0)
        rt = pltpu.roll(c, wp - 1, 0)
        nb = (up + dn) + (lf + rt)
        v = (alpha * c + beta * nb) + (b_ref[pl.ds(o, wp), :] - m_ref[pl.ds(o - wp, wp), :])
        return jnp.maximum(v, 0.0)

    m_ref[...] = jnp.dot(f3_ref[pl.ds(2 * wp, inner), :], g3_ref[...],
                         preferred_element_type=jnp.float32)

    def body1(q, carry):
        f1 = update(f0_ref, q) * cm
        f1_ref[pl.ds(pl.multiple_of(q * wp, 8), wp), :] = f1
        return carry

    lax.fori_loop(1, rows - 1, body1, 0, unroll=2)
    for q in (1, rows - 2):
        f1_ref[pl.ds(q * wp, wp), :] = f1_ref[pl.ds(q * wp, wp), :] * rm_ref[t * TR + q]

    f3_ref[pl.ds(2 * wp, inner), :] = f1_ref[pl.ds(wp, inner), :].astype(jnp.bfloat16)
    m_ref[...] = jnp.dot(f3_ref[pl.ds(2 * wp, inner), :], g3_ref[...],
                         preferred_element_type=jnp.float32)

    def body2(q, carry):
        f2 = update(f1_ref, q)
        f2 = pltpu.roll(f2, wp - CH, 0)
        o_ref[0, q - RH] = f2[: wp - 2 * CH]
        return carry

    lax.fori_loop(RH, rows - RH, body2, 0, unroll=2)


def pin(x):
    return with_layout_constraint(x, Layout(tuple(range(x.ndim))))


def per_device(images, rates, smoothing):
    kernel, gram, lam, step = kernel_parts(rates, smoothing)
    kb = kernel.astype(jnp.bfloat16)
    g3 = (gram * step[None, :]).astype(jnp.bfloat16)
    beta = step * lam
    alpha = 1.0 - 4.0 * beta
    x = lax.all_to_all(images, "gy", split_axis=3, concat_axis=0, tiled=True)
    e, sl, h, w = x.shape
    hp, wp = h + 2 * RH, w + 2 * CH
    x = pin(jnp.transpose(x, (1, 2, 3, 0)))
    x = pin(halo(x, "gy", 2, CH))
    x = pin(halo(x, "gx", 1, RH))
    r = kernel.shape[1]

    gi = lax.axis_index("gx")
    gj = lax.axis_index("gy")
    grow = gi * h + jnp.arange(hp) - RH
    rm = ((grow >= 0) & (grow < h * lax.axis_size("gx"))).astype(jnp.float32)
    gcol = gj * w + jnp.arange(wp) - CH
    cv = ((gcol >= 0) & (gcol < w * lax.axis_size("gy"))).astype(jnp.float32)
    cm = jnp.broadcast_to(cv[:, None], (wp, r))

    rows = TR + 2 * RH
    nt = h // TR
    flops = 2 * sl * nt * rows * wp * r * (e + 2 * r)
    out = pl.pallas_call(
        functools.partial(fit_kernel, wp),
        out_shape=jax.ShapeDtypeStruct((sl, h, w, r), jnp.float32),
        grid=(sl, nt),
        in_specs=[
            pl.BlockSpec((1, hp, wp, e), lambda s, t: (s, 0, 0, 0)),
            pl.BlockSpec((e, r), lambda s, t: (0, 0)),
            pl.BlockSpec((r, r), lambda s, t: (0, 0)),
            pl.BlockSpec((1, r), lambda s, t: (0, 0)),
            pl.BlockSpec((1, r), lambda s, t: (0, 0)),
            pl.BlockSpec((1, r), lambda s, t: (0, 0)),
            pl.BlockSpec((wp, r), lambda s, t: (0, 0)),
            pl.BlockSpec(memory_space=pltpu.SMEM),
        ],
        out_specs=pl.BlockSpec((1, TR, w, r), lambda s, t: (s, t, 0, 0)),
        scratch_shapes=[
            pltpu.VMEM((rows * wp, r), jnp.float32),
            pltpu.VMEM((rows * wp, r), jnp.float32),
            pltpu.VMEM((rows * wp, r), jnp.float32),
            pltpu.VMEM((rows * wp, r), jnp.bfloat16),
            pltpu.VMEM(((rows - 2) * wp, r), jnp.float32),
        ],
        compiler_params=pltpu.CompilerParams(
            dimension_semantics=("arbitrary", "arbitrary"),
            vmem_limit_bytes=48 * 1024 * 1024,
        ),
        cost_estimate=pl.CostEstimate(
            flops=flops, transcendentals=0,
            bytes_accessed=sl * (hp * wp * e * 2 + h * w * r * 4),
        ),
    )(x, kb, g3, step[None, :], alpha[None, :], beta[None, :], cm, rm)
    return out


def solution(mesh):
    in_specs = (P("gy", None, "gx", None), P(), P())
    out_specs = P(None, "gx", "gy", None)
    return jax.shard_map(
        per_device, mesh=mesh, in_specs=in_specs, out_specs=out_specs, check_vma=False
    )
```

```python
import functools

import jax
import jax.numpy as jnp
from jax import lax
from jax.experimental import pallas as pl
from jax.experimental.pallas import tpu as pltpu
from jax.experimental.layout import Layout, with_layout_constraint
from jax.sharding import PartitionSpec as P

E = 64
ITERS = 3
RH = 2
CH = 4
TR = 64


def kernel_parts(rates, smoothing):
    times = 10.0 * (jnp.arange(E, dtype=jnp.float32) + 1.0)
    raw = jnp.exp(-times[:, None] * rates[None, :])
    kernel = raw / jnp.sqrt(jnp.sum(raw * raw, axis=0))[None, :]
    gram = jnp.dot(kernel.T, kernel, precision=lax.Precision.HIGHEST)
    rowsum = jnp.sum(gram, axis=1)
    lam = smoothing * rowsum
    step = 1.0 / (rowsum + 8.0 * lam)
    return (kernel, gram, lam, step)


def halo(cells, axis, dim, width):
    count = lax.axis_size(axis)
    head = lax.slice_in_dim(cells, 0, width, axis=dim)
    tail = lax.slice_in_dim(cells, cells.shape[dim] - width, cells.shape[dim], axis=dim)
    return jnp.concatenate(
        [
            lax.ppermute(tail, axis, [(i, i + 1) for i in range(count - 1)]),
            cells,
            lax.ppermute(head, axis, [(i + 1, i) for i in range(count - 1)]),
        ],
        axis=dim,
    )


def fit_kernel(wp, x_ref, kb_ref, g3_ref, step_ref, alpha_ref, beta_ref, cm_ref, rm_ref,
               o_ref, b_ref, f0_ref, f1_ref, f3_ref, m_ref):
    t = pl.program_id(1)
    rows = TR + 2 * RH
    n = rows * wp
    base = pl.multiple_of(t * (TR * wp), 16)
    step = step_ref[...]
    alpha = alpha_ref[...]
    beta = beta_ref[...]
    cm = cm_ref[...]

    xt = x_ref[0, pl.ds(t * TR, rows)].astype(jnp.float32).reshape(n, x_ref.shape[3])
    sb = jnp.dot(xt.astype(jnp.bfloat16), kb_ref[...],
                 preferred_element_type=jnp.float32) * step
    b_ref[...] = sb
    f0 = jnp.maximum(sb, 0.0)
    f0_ref[...] = f0
    inner = (rows - 2) * wp
    f3_ref[pl.ds(2 * wp, inner), :] = f0[wp:(rows - 1) * wp].astype(jnp.bfloat16)

    def update(src_ref, q):
        o = pl.multiple_of(q * wp, 8)
        c = src_ref[pl.ds(o, wp), :]
        up = src_ref[pl.ds(o - wp, wp), :]
        dn = src_ref[pl.ds(o + wp, wp), :]
        lf = pltpu.roll(c, 1, 0)
        rt = pltpu.roll(c, wp - 1, 0)
        nb = (up + dn) + (lf + rt)
        v = (alpha * c + beta * nb) + (b_ref[pl.ds(o, wp), :] - m_ref[pl.ds(o - wp, wp), :])
        return jnp.maximum(v, 0.0)

    m_ref[...] = jnp.dot(f3_ref[pl.ds(2 * wp, inner), :], g3_ref[...],
                         preferred_element_type=jnp.float32)

    def body1(q, carry):
        f1 = update(f0_ref, q) * cm
        f1_ref[pl.ds(pl.multiple_of(q * wp, 8), wp), :] = f1
        return carry

    lax.fori_loop(1, rows - 1, body1, 0, unroll=4)
    for q in (1, rows - 2):
        f1_ref[pl.ds(q * wp, wp), :] = f1_ref[pl.ds(q * wp, wp), :] * rm_ref[t * TR + q]

    f3_ref[pl.ds(2 * wp, inner), :] = f1_ref[pl.ds(wp, inner), :].astype(jnp.bfloat16)
    m_ref[...] = jnp.dot(f3_ref[pl.ds(2 * wp, inner), :], g3_ref[...],
                         preferred_element_type=jnp.float32)

    def body2(q, carry):
        f2 = update(f1_ref, q)
        f2 = pltpu.roll(f2, wp - CH, 0)
        o_ref[0, q - RH] = f2[: wp - 2 * CH]
        return carry

    lax.fori_loop(RH, rows - RH, body2, 0, unroll=4)


def pin(x):
    return with_layout_constraint(x, Layout(tuple(range(x.ndim))))


def per_device(images, rates, smoothing):
    kernel, gram, lam, step = kernel_parts(rates, smoothing)
    kb = kernel.astype(jnp.bfloat16)
    g3 = (gram * step[None, :]).astype(jnp.bfloat16)
    beta = step * lam
    alpha = 1.0 - 4.0 * beta
    x = lax.all_to_all(images, "gy", split_axis=3, concat_axis=0, tiled=True)
    e, sl, h, w = x.shape
    hp, wp = h + 2 * RH, w + 2 * CH
    x = pin(jnp.transpose(x, (1, 2, 3, 0)))
    x = pin(halo(x, "gy", 2, CH))
    x = pin(halo(x, "gx", 1, RH))
    r = kernel.shape[1]

    gi = lax.axis_index("gx")
    gj = lax.axis_index("gy")
    grow = gi * h + jnp.arange(hp) - RH
    rm = ((grow >= 0) & (grow < h * lax.axis_size("gx"))).astype(jnp.float32)
    gcol = gj * w + jnp.arange(wp) - CH
    cv = ((gcol >= 0) & (gcol < w * lax.axis_size("gy"))).astype(jnp.float32)
    cm = jnp.broadcast_to(cv[:, None], (wp, r))

    rows = TR + 2 * RH
    nt = h // TR
    flops = 2 * sl * nt * rows * wp * r * (e + 2 * r)
    out = pl.pallas_call(
        functools.partial(fit_kernel, wp),
        out_shape=jax.ShapeDtypeStruct((sl, h, w, r), jnp.float32),
        grid=(sl, nt),
        in_specs=[
            pl.BlockSpec((1, hp, wp, e), lambda s, t: (s, 0, 0, 0)),
            pl.BlockSpec((e, r), lambda s, t: (0, 0)),
            pl.BlockSpec((r, r), lambda s, t: (0, 0)),
            pl.BlockSpec((1, r), lambda s, t: (0, 0)),
            pl.BlockSpec((1, r), lambda s, t: (0, 0)),
            pl.BlockSpec((1, r), lambda s, t: (0, 0)),
            pl.BlockSpec((wp, r), lambda s, t: (0, 0)),
            pl.BlockSpec(memory_space=pltpu.SMEM),
        ],
        out_specs=pl.BlockSpec((1, TR, w, r), lambda s, t: (s, t, 0, 0)),
        scratch_shapes=[
            pltpu.VMEM((rows * wp, r), jnp.float32),
            pltpu.VMEM((rows * wp, r), jnp.float32),
            pltpu.VMEM((rows * wp, r), jnp.float32),
            pltpu.VMEM((rows * wp, r), jnp.bfloat16),
            pltpu.VMEM(((rows - 2) * wp, r), jnp.float32),
        ],
        compiler_params=pltpu.CompilerParams(
            dimension_semantics=("arbitrary", "arbitrary"),
            vmem_limit_bytes=48 * 1024 * 1024,
        ),
        cost_estimate=pl.CostEstimate(
            flops=flops, transcendentals=0,
            bytes_accessed=sl * (hp * wp * e * 2 + h * w * r * 4),
        ),
    )(x, kb, g3, step[None, :], alpha[None, :], beta[None, :], cm, rm)
    return out


def solution(mesh):
    in_specs = (P("gy", None, "gx", None), P(), P())
    out_specs = P(None, "gx", "gy", None)
    return jax.shard_map(
        per_device, mesh=mesh, in_specs=in_specs, out_specs=out_specs, check_vma=False
    )
```

```python
import functools

import jax
import jax.numpy as jnp
from jax import lax
from jax.experimental import pallas as pl
from jax.experimental.pallas import tpu as pltpu
from jax.experimental.layout import Layout, with_layout_constraint
from jax.sharding import PartitionSpec as P

E = 64
ITERS = 3
RH = 2
CH = 4
TR = 64


def kernel_parts(rates, smoothing):
    times = 10.0 * (jnp.arange(E, dtype=jnp.float32) + 1.0)
    raw = jnp.exp(-times[:, None] * rates[None, :])
    kernel = raw / jnp.sqrt(jnp.sum(raw * raw, axis=0))[None, :]
    gram = jnp.dot(kernel.T, kernel, precision=lax.Precision.HIGHEST)
    rowsum = jnp.sum(gram, axis=1)
    lam = smoothing * rowsum
    step = 1.0 / (rowsum + 8.0 * lam)
    return (kernel, gram, lam, step)


def halo(cells, axis, dim, width):
    count = lax.axis_size(axis)
    head = lax.slice_in_dim(cells, 0, width, axis=dim)
    tail = lax.slice_in_dim(cells, cells.shape[dim] - width, cells.shape[dim], axis=dim)
    return jnp.concatenate(
        [
            lax.ppermute(tail, axis, [(i, i + 1) for i in range(count - 1)]),
            cells,
            lax.ppermute(head, axis, [(i + 1, i) for i in range(count - 1)]),
        ],
        axis=dim,
    )


def fit_kernel(wp, x_ref, kb_ref, g3_ref, step_ref, alpha_ref, beta_ref, cm_ref, rm_ref,
               o_ref, b_ref, f0_ref, f1_ref, f3_ref, m_ref):
    t = pl.program_id(1)
    rows = TR + 2 * RH
    n = rows * wp
    base = pl.multiple_of(t * (TR * wp), 16)
    step = step_ref[...]
    alpha = alpha_ref[...]
    beta = beta_ref[...]
    cm = cm_ref[...]

    xt = x_ref[0, pl.ds(t * TR, rows)].astype(jnp.float32).reshape(n, x_ref.shape[3])
    sb = jnp.dot(xt.astype(jnp.bfloat16), kb_ref[...],
                 preferred_element_type=jnp.float32) * step
    b_ref[...] = sb
    f0 = jnp.maximum(sb, 0.0)
    f0_ref[...] = f0
    inner = (rows - 2) * wp
    f3_ref[pl.ds(2 * wp, inner), :] = f0[wp:(rows - 1) * wp].astype(jnp.bfloat16)

    def update(src_ref, q):
        o = pl.multiple_of(q * wp, 8)
        c = src_ref[pl.ds(o, wp), :]
        up = src_ref[pl.ds(o - wp, wp), :]
        dn = src_ref[pl.ds(o + wp, wp), :]
        lf = pltpu.roll(c, 1, 0)
        rt = pltpu.roll(c, wp - 1, 0)
        nb = (up + dn) + (lf + rt)
        v = (alpha * c + beta * nb) + (b_ref[pl.ds(o, wp), :] - m_ref[pl.ds(o - wp, wp), :])
        return jnp.maximum(v, 0.0)

    m_ref[...] = jnp.dot(f3_ref[pl.ds(2 * wp, inner), :], g3_ref[...],
                         preferred_element_type=jnp.float32)

    def body1(q, carry):
        f1 = update(f0_ref, q) * cm
        f1_ref[pl.ds(pl.multiple_of(q * wp, 8), wp), :] = f1
        return carry

    lax.fori_loop(1, rows - 1, body1, 0, unroll=2)
    for q in (1, rows - 2):
        f1_ref[pl.ds(q * wp, wp), :] = f1_ref[pl.ds(q * wp, wp), :] * rm_ref[t * TR + q]

    f3_ref[pl.ds(2 * wp, inner), :] = f1_ref[pl.ds(wp, inner), :].astype(jnp.bfloat16)
    m_ref[...] = jnp.dot(f3_ref[pl.ds(2 * wp, inner), :], g3_ref[...],
                         preferred_element_type=jnp.float32)

    def body2(q, carry):
        f2 = update(f1_ref, q)
        f2 = pltpu.roll(f2, wp - CH, 0)
        o_ref[0, q - RH] = f2[: wp - 2 * CH]
        return carry

    lax.fori_loop(RH, rows - RH, body2, 0, unroll=2)


def pin(x):
    return with_layout_constraint(x, Layout(tuple(range(x.ndim))))


def per_device(images, rates, smoothing):
    kernel, gram, lam, step = kernel_parts(rates, smoothing)
    kb = kernel.astype(jnp.bfloat16)
    g3 = (gram * step[None, :]).astype(jnp.bfloat16)
    beta = step * lam
    alpha = 1.0 - 4.0 * beta
    x = lax.all_to_all(images, "gy", split_axis=3, concat_axis=0, tiled=True)
    e, sl, h, w = x.shape
    hp, wp = h + 2 * RH, w + 2 * CH
    ny = lax.axis_size("gy")
    dense = Layout((3, 1, 0, 2))
    head = with_layout_constraint(x[..., :CH], dense)
    tail = with_layout_constraint(x[..., w - CH:], dense)
    left = lax.ppermute(tail, "gy", [(i, i + 1) for i in range(ny - 1)])
    right = lax.ppermute(head, "gy", [(i + 1, i) for i in range(ny - 1)])
    x = jnp.concatenate([pin(jnp.transpose(left, (1, 2, 3, 0))),
                         pin(jnp.transpose(x, (1, 2, 3, 0))),
                         pin(jnp.transpose(right, (1, 2, 3, 0)))], axis=2)
    x = pin(x)
    x = pin(halo(x, "gx", 1, RH))
    r = kernel.shape[1]

    gi = lax.axis_index("gx")
    gj = lax.axis_index("gy")
    grow = gi * h + jnp.arange(hp) - RH
    rm = ((grow >= 0) & (grow < h * lax.axis_size("gx"))).astype(jnp.float32)
    gcol = gj * w + jnp.arange(wp) - CH
    cv = ((gcol >= 0) & (gcol < w * lax.axis_size("gy"))).astype(jnp.float32)
    cm = jnp.broadcast_to(cv[:, None], (wp, r))

    rows = TR + 2 * RH
    nt = h // TR
    flops = 2 * sl * nt * rows * wp * r * (e + 2 * r)
    out = pl.pallas_call(
        functools.partial(fit_kernel, wp),
        out_shape=jax.ShapeDtypeStruct((sl, h, w, r), jnp.float32),
        grid=(sl, nt),
        in_specs=[
            pl.BlockSpec((1, hp, wp, e), lambda s, t: (s, 0, 0, 0)),
            pl.BlockSpec((e, r), lambda s, t: (0, 0)),
            pl.BlockSpec((r, r), lambda s, t: (0, 0)),
            pl.BlockSpec((1, r), lambda s, t: (0, 0)),
            pl.BlockSpec((1, r), lambda s, t: (0, 0)),
            pl.BlockSpec((1, r), lambda s, t: (0, 0)),
            pl.BlockSpec((wp, r), lambda s, t: (0, 0)),
            pl.BlockSpec(memory_space=pltpu.SMEM),
        ],
        out_specs=pl.BlockSpec((1, TR, w, r), lambda s, t: (s, t, 0, 0)),
        scratch_shapes=[
            pltpu.VMEM((rows * wp, r), jnp.float32),
            pltpu.VMEM((rows * wp, r), jnp.float32),
            pltpu.VMEM((rows * wp, r), jnp.float32),
            pltpu.VMEM((rows * wp, r), jnp.bfloat16),
            pltpu.VMEM(((rows - 2) * wp, r), jnp.float32),
        ],
        compiler_params=pltpu.CompilerParams(
            dimension_semantics=("arbitrary", "arbitrary"),
            vmem_limit_bytes=48 * 1024 * 1024,
        ),
        cost_estimate=pl.CostEstimate(
            flops=flops, transcendentals=0,
            bytes_accessed=sl * (hp * wp * e * 2 + h * w * r * 4),
        ),
    )(x, kb, g3, step[None, :], alpha[None, :], beta[None, :], cm, rm)
    return out


def solution(mesh):
    in_specs = (P("gy", None, "gx", None), P(), P())
    out_specs = P(None, "gx", "gy", None)
    return jax.shard_map(
        per_device, mesh=mesh, in_specs=in_specs, out_specs=out_specs, check_vma=False
    )
```

```python
import functools

import jax
import jax.numpy as jnp
from jax import lax
from jax.experimental import pallas as pl
from jax.experimental.pallas import tpu as pltpu
from jax.experimental.layout import Layout, with_layout_constraint
from jax.sharding import PartitionSpec as P

E = 64
ITERS = 3
RH = 2
CH = 4
TR = 64


def kernel_parts(rates, smoothing):
    times = 10.0 * (jnp.arange(E, dtype=jnp.float32) + 1.0)
    raw = jnp.exp(-times[:, None] * rates[None, :])
    kernel = raw / jnp.sqrt(jnp.sum(raw * raw, axis=0))[None, :]
    gram = jnp.dot(kernel.T, kernel, precision=lax.Precision.HIGHEST)
    rowsum = jnp.sum(gram, axis=1)
    lam = smoothing * rowsum
    step = 1.0 / (rowsum + 8.0 * lam)
    return (kernel, gram, lam, step)


def halo(cells, axis, dim, width):
    count = lax.axis_size(axis)
    head = lax.slice_in_dim(cells, 0, width, axis=dim)
    tail = lax.slice_in_dim(cells, cells.shape[dim] - width, cells.shape[dim], axis=dim)
    return jnp.concatenate(
        [
            lax.ppermute(tail, axis, [(i, i + 1) for i in range(count - 1)]),
            cells,
            lax.ppermute(head, axis, [(i + 1, i) for i in range(count - 1)]),
        ],
        axis=dim,
    )


def fit_kernel(wp, x_ref, kb_ref, g3_ref, step_ref, alpha_ref, beta_ref, cm_ref, rm_ref,
               o_ref, b_ref, f0_ref, f1_ref, f3_ref, m_ref):
    t = pl.program_id(1)
    rows = TR + 2 * RH
    n = rows * wp
    base = pl.multiple_of(t * (TR * wp), 16)
    step = step_ref[...]
    alpha = alpha_ref[...]
    beta = beta_ref[...]
    cm = cm_ref[...]

    xt = x_ref[0, pl.ds(t * TR, rows)].astype(jnp.float32).reshape(n, x_ref.shape[3])
    sb = jnp.dot(xt.astype(jnp.bfloat16), kb_ref[...],
                 preferred_element_type=jnp.float32) * step
    b_ref[...] = sb
    f0 = jnp.maximum(sb, 0.0)
    f0_ref[...] = f0
    inner = (rows - 2) * wp
    f3_ref[pl.ds(2 * wp, inner), :] = f0[wp:(rows - 1) * wp].astype(jnp.bfloat16)

    def update(src_ref, q):
        o = pl.multiple_of(q * wp, 8)
        c = src_ref[pl.ds(o, wp), :]
        up = src_ref[pl.ds(o - wp, wp), :]
        dn = src_ref[pl.ds(o + wp, wp), :]
        lf = pltpu.roll(c, 1, 0)
        rt = pltpu.roll(c, wp - 1, 0)
        nb = (up + dn) + (lf + rt)
        v = (alpha * c + beta * nb) + (b_ref[pl.ds(o, wp), :] - m_ref[pl.ds(o - wp, wp), :])
        return jnp.maximum(v, 0.0)

    m_ref[...] = jnp.dot(f3_ref[pl.ds(2 * wp, inner), :], g3_ref[...],
                         preferred_element_type=jnp.float32)

    def body1(q, carry):
        f1 = update(f0_ref, q) * cm
        f1_ref[pl.ds(pl.multiple_of(q * wp, 8), wp), :] = f1
        return carry

    lax.fori_loop(1, rows - 1, body1, 0, unroll=2)
    for q in (1, rows - 2):
        f1_ref[pl.ds(q * wp, wp), :] = f1_ref[pl.ds(q * wp, wp), :] * rm_ref[t * TR + q]

    f3_ref[pl.ds(2 * wp, inner), :] = f1_ref[pl.ds(wp, inner), :].astype(jnp.bfloat16)
    m_ref[...] = jnp.dot(f3_ref[pl.ds(2 * wp, inner), :], g3_ref[...],
                         preferred_element_type=jnp.float32)

    def body2(q, carry):
        f2 = update(f1_ref, q)
        f2 = pltpu.roll(f2, wp - CH, 0)
        o_ref[0, q - RH] = f2[: wp - 2 * CH]
        return carry

    lax.fori_loop(RH, rows - RH, body2, 0, unroll=2)


def pin(x):
    return with_layout_constraint(x, Layout(tuple(range(x.ndim))))


def per_device(images, rates, smoothing):
    kernel, gram, lam, step = kernel_parts(rates, smoothing)
    kb = kernel.astype(jnp.bfloat16)
    g3 = (gram * step[None, :]).astype(jnp.bfloat16)
    beta = step * lam
    alpha = 1.0 - 4.0 * beta
    x = lax.all_to_all(images, "gy", split_axis=3, concat_axis=0, tiled=True)
    e, sl, h, w = x.shape
    hp, wp = h + 2 * RH, w + 2 * CH
    ny = lax.axis_size("gy")
    dense = Layout((3, 1, 0, 2))
    head = with_layout_constraint(x[..., :CH], dense)
    tail = with_layout_constraint(x[..., w - CH:], dense)
    left = lax.ppermute(tail, "gy", [(i, i + 1) for i in range(ny - 1)])
    right = lax.ppermute(head, "gy", [(i + 1, i) for i in range(ny - 1)])
    nx = lax.axis_size("gx")
    edge = lambda a, b: jnp.concatenate([left[:, :, a:b], x[:, :, a:b], right[:, :, a:b]], axis=3)
    top = lax.ppermute(edge(h - RH, h), "gx", [(i, i + 1) for i in range(nx - 1)])
    bot = lax.ppermute(edge(0, RH), "gx", [(i + 1, i) for i in range(nx - 1)])
    em = lambda a: pin(jnp.transpose(a, (1, 2, 3, 0)))
    centre = jnp.concatenate([pin(jnp.transpose(x[:, k:k + 1], (1, 2, 3, 0)))
                              for k in range(sl)], axis=0)
    mid = jnp.concatenate([em(left), centre, em(right)], axis=2)
    x = pin(jnp.concatenate([em(top), mid, em(bot)], axis=1))
    r = kernel.shape[1]

    gi = lax.axis_index("gx")
    gj = lax.axis_index("gy")
    grow = gi * h + jnp.arange(hp) - RH
    rm = ((grow >= 0) & (grow < h * lax.axis_size("gx"))).astype(jnp.float32)
    gcol = gj * w + jnp.arange(wp) - CH
    cv = ((gcol >= 0) & (gcol < w * lax.axis_size("gy"))).astype(jnp.float32)
    cm = jnp.broadcast_to(cv[:, None], (wp, r))

    rows = TR + 2 * RH
    nt = h // TR
    flops = 2 * sl * nt * rows * wp * r * (e + 2 * r)
    out = pl.pallas_call(
        functools.partial(fit_kernel, wp),
        out_shape=jax.ShapeDtypeStruct((sl, h, w, r), jnp.float32),
        grid=(sl, nt),
        in_specs=[
            pl.BlockSpec((1, hp, wp, e), lambda s, t: (s, 0, 0, 0)),
            pl.BlockSpec((e, r), lambda s, t: (0, 0)),
            pl.BlockSpec((r, r), lambda s, t: (0, 0)),
            pl.BlockSpec((1, r), lambda s, t: (0, 0)),
            pl.BlockSpec((1, r), lambda s, t: (0, 0)),
            pl.BlockSpec((1, r), lambda s, t: (0, 0)),
            pl.BlockSpec((wp, r), lambda s, t: (0, 0)),
            pl.BlockSpec(memory_space=pltpu.SMEM),
        ],
        out_specs=pl.BlockSpec((1, TR, w, r), lambda s, t: (s, t, 0, 0)),
        scratch_shapes=[
            pltpu.VMEM((rows * wp, r), jnp.float32),
            pltpu.VMEM((rows * wp, r), jnp.float32),
            pltpu.VMEM((rows * wp, r), jnp.float32),
            pltpu.VMEM((rows * wp, r), jnp.bfloat16),
            pltpu.VMEM(((rows - 2) * wp, r), jnp.float32),
        ],
        compiler_params=pltpu.CompilerParams(
            dimension_semantics=("arbitrary", "arbitrary"),
            vmem_limit_bytes=48 * 1024 * 1024,
        ),
        cost_estimate=pl.CostEstimate(
            flops=flops, transcendentals=0,
            bytes_accessed=sl * (hp * wp * e * 2 + h * w * r * 4),
        ),
    )(x, kb, g3, step[None, :], alpha[None, :], beta[None, :], cm, rm)
    return out


def solution(mesh):
    in_specs = (P("gy", None, "gx", None), P(), P())
    out_specs = P(None, "gx", "gy", None)
    return jax.shard_map(
        per_device, mesh=mesh, in_specs=in_specs, out_specs=out_specs, check_vma=False
    )
```

```python
import functools

import jax
import jax.numpy as jnp
from jax import lax
from jax.experimental import pallas as pl
from jax.experimental.pallas import tpu as pltpu
from jax.experimental.layout import Layout, with_layout_constraint
from jax.sharding import PartitionSpec as P

E = 64
ITERS = 3
RH = 2
CH = 4
TR = 64


def kernel_parts(rates, smoothing):
    times = 10.0 * (jnp.arange(E, dtype=jnp.float32) + 1.0)
    raw = jnp.exp(-times[:, None] * rates[None, :])
    kernel = raw / jnp.sqrt(jnp.sum(raw * raw, axis=0))[None, :]
    gram = jnp.dot(kernel.T, kernel, precision=lax.Precision.HIGHEST)
    rowsum = jnp.sum(gram, axis=1)
    lam = smoothing * rowsum
    step = 1.0 / (rowsum + 8.0 * lam)
    return (kernel, gram, lam, step)


def halo(cells, axis, dim, width):
    count = lax.axis_size(axis)
    head = lax.slice_in_dim(cells, 0, width, axis=dim)
    tail = lax.slice_in_dim(cells, cells.shape[dim] - width, cells.shape[dim], axis=dim)
    return jnp.concatenate(
        [
            lax.ppermute(tail, axis, [(i, i + 1) for i in range(count - 1)]),
            cells,
            lax.ppermute(head, axis, [(i + 1, i) for i in range(count - 1)]),
        ],
        axis=dim,
    )


def fit_kernel(wp, x_ref, kb_ref, g3_ref, step_ref, alpha_ref, beta_ref, cm_ref, rm_ref,
               o_ref, b_ref, f0_ref, f1_ref, f3_ref, m_ref):
    t = pl.program_id(1)
    rows = TR + 2 * RH
    n = rows * wp
    base = pl.multiple_of(t * (TR * wp), 16)
    step = step_ref[...]
    alpha = alpha_ref[...]
    beta = beta_ref[...]
    cm = cm_ref[...]

    xt = x_ref[0, pl.ds(t * TR, rows)].astype(jnp.float32).reshape(n, x_ref.shape[3])
    sb = jnp.dot(xt.astype(jnp.bfloat16), kb_ref[...],
                 preferred_element_type=jnp.float32) * step
    b_ref[...] = sb
    f0 = jnp.maximum(sb, 0.0)
    f0_ref[...] = f0
    inner = (rows - 2) * wp
    f3_ref[pl.ds(2 * wp, inner), :] = f0[wp:(rows - 1) * wp].astype(jnp.bfloat16)

    def update(src_ref, q, mo):
        o = pl.multiple_of(q * wp, 8)
        c = src_ref[pl.ds(o, wp), :]
        up = src_ref[pl.ds(o - wp, wp), :]
        dn = src_ref[pl.ds(o + wp, wp), :]
        lf = pltpu.roll(c, 1, 0)
        rt = pltpu.roll(c, wp - 1, 0)
        nb = (up + dn) + (lf + rt)
        v = (alpha * c + beta * nb) + (b_ref[pl.ds(o, wp), :] - m_ref[pl.ds(o - mo * wp, wp), :])
        return jnp.maximum(v, 0.0)

    m_ref[...] = jnp.dot(f3_ref[pl.ds(2 * wp, inner), :], g3_ref[...],
                         preferred_element_type=jnp.float32)

    def body1(q, carry):
        f1 = update(f0_ref, q, 1) * cm
        f1_ref[pl.ds(pl.multiple_of(q * wp, 8), wp), :] = f1
        return carry

    lax.fori_loop(1, rows - 1, body1, 0, unroll=2)
    for q in (1, rows - 2):
        f1_ref[pl.ds(q * wp, wp), :] = f1_ref[pl.ds(q * wp, wp), :] * rm_ref[t * TR + q]

    inner2 = (rows - 4) * wp
    f3_ref[pl.ds(2 * wp, inner2), :] = f1_ref[pl.ds(2 * wp, inner2), :].astype(jnp.bfloat16)
    m_ref[pl.ds(0, inner2), :] = jnp.dot(f3_ref[pl.ds(2 * wp, inner2), :], g3_ref[...],
                                         preferred_element_type=jnp.float32)

    def body2(q, carry):
        f2 = update(f1_ref, q, 2)
        f2 = pltpu.roll(f2, wp - CH, 0)
        o_ref[0, q - RH] = f2[: wp - 2 * CH]
        return carry

    lax.fori_loop(RH, rows - RH, body2, 0, unroll=2)


def pin(x):
    return with_layout_constraint(x, Layout(tuple(range(x.ndim))))


def per_device(images, rates, smoothing):
    kernel, gram, lam, step = kernel_parts(rates, smoothing)
    kb = kernel.astype(jnp.bfloat16)
    g3 = (gram * step[None, :]).astype(jnp.bfloat16)
    beta = step * lam
    alpha = 1.0 - 4.0 * beta
    x = lax.all_to_all(images, "gy", split_axis=3, concat_axis=0, tiled=True)
    e, sl, h, w = x.shape
    hp, wp = h + 2 * RH, w + 2 * CH
    ny = lax.axis_size("gy")
    dense = Layout((3, 1, 0, 2))
    head = with_layout_constraint(x[..., :CH], dense)
    tail = with_layout_constraint(x[..., w - CH:], dense)
    left = lax.ppermute(tail, "gy", [(i, i + 1) for i in range(ny - 1)])
    right = lax.ppermute(head, "gy", [(i + 1, i) for i in range(ny - 1)])
    x = jnp.concatenate([pin(jnp.transpose(left, (1, 2, 3, 0))),
                         pin(jnp.transpose(x, (1, 2, 3, 0))),
                         pin(jnp.transpose(right, (1, 2, 3, 0)))], axis=2)
    x = pin(x)
    x = pin(halo(x, "gx", 1, RH))
    r = kernel.shape[1]

    gi = lax.axis_index("gx")
    gj = lax.axis_index("gy")
    grow = gi * h + jnp.arange(hp) - RH
    rm = ((grow >= 0) & (grow < h * lax.axis_size("gx"))).astype(jnp.float32)
    gcol = gj * w + jnp.arange(wp) - CH
    cv = ((gcol >= 0) & (gcol < w * lax.axis_size("gy"))).astype(jnp.float32)
    cm = jnp.broadcast_to(cv[:, None], (wp, r))

    rows = TR + 2 * RH
    nt = h // TR
    flops = 2 * sl * nt * rows * wp * r * (e + 2 * r)
    out = pl.pallas_call(
        functools.partial(fit_kernel, wp),
        out_shape=jax.ShapeDtypeStruct((sl, h, w, r), jnp.float32),
        grid=(sl, nt),
        in_specs=[
            pl.BlockSpec((1, hp, wp, e), lambda s, t: (s, 0, 0, 0)),
            pl.BlockSpec((e, r), lambda s, t: (0, 0)),
            pl.BlockSpec((r, r), lambda s, t: (0, 0)),
            pl.BlockSpec((1, r), lambda s, t: (0, 0)),
            pl.BlockSpec((1, r), lambda s, t: (0, 0)),
            pl.BlockSpec((1, r), lambda s, t: (0, 0)),
            pl.BlockSpec((wp, r), lambda s, t: (0, 0)),
            pl.BlockSpec(memory_space=pltpu.SMEM),
        ],
        out_specs=pl.BlockSpec((1, TR, w, r), lambda s, t: (s, t, 0, 0)),
        scratch_shapes=[
            pltpu.VMEM((rows * wp, r), jnp.float32),
            pltpu.VMEM((rows * wp, r), jnp.float32),
            pltpu.VMEM((rows * wp, r), jnp.float32),
            pltpu.VMEM((rows * wp, r), jnp.bfloat16),
            pltpu.VMEM(((rows - 2) * wp, r), jnp.float32),
        ],
        compiler_params=pltpu.CompilerParams(
            dimension_semantics=("arbitrary", "arbitrary"),
            vmem_limit_bytes=48 * 1024 * 1024,
        ),
        cost_estimate=pl.CostEstimate(
            flops=flops, transcendentals=0,
            bytes_accessed=sl * (hp * wp * e * 2 + h * w * r * 4),
        ),
    )(x, kb, g3, step[None, :], alpha[None, :], beta[None, :], cm, rm)
    return out


def solution(mesh):
    in_specs = (P("gy", None, "gx", None), P(), P())
    out_specs = P(None, "gx", "gy", None)
    return jax.shard_map(
        per_device, mesh=mesh, in_specs=in_specs, out_specs=out_specs, check_vma=False
    )
```

```python
import functools

import jax
import jax.numpy as jnp
from jax import lax
from jax.experimental import pallas as pl
from jax.experimental.pallas import tpu as pltpu
from jax.experimental.layout import Layout, with_layout_constraint
from jax.sharding import PartitionSpec as P

E = 64
ITERS = 3
RH = 2
CH = 4
TR = 32


def kernel_parts(rates, smoothing):
    times = 10.0 * (jnp.arange(E, dtype=jnp.float32) + 1.0)
    raw = jnp.exp(-times[:, None] * rates[None, :])
    kernel = raw / jnp.sqrt(jnp.sum(raw * raw, axis=0))[None, :]
    gram = jnp.dot(kernel.T, kernel, precision=lax.Precision.HIGHEST)
    rowsum = jnp.sum(gram, axis=1)
    lam = smoothing * rowsum
    step = 1.0 / (rowsum + 8.0 * lam)
    return (kernel, gram, lam, step)


def halo(cells, axis, dim, width):
    count = lax.axis_size(axis)
    head = lax.slice_in_dim(cells, 0, width, axis=dim)
    tail = lax.slice_in_dim(cells, cells.shape[dim] - width, cells.shape[dim], axis=dim)
    return jnp.concatenate(
        [
            lax.ppermute(tail, axis, [(i, i + 1) for i in range(count - 1)]),
            cells,
            lax.ppermute(head, axis, [(i + 1, i) for i in range(count - 1)]),
        ],
        axis=dim,
    )


def fit_kernel(wp, x_ref, kb_ref, g3_ref, step_ref, alpha_ref, beta_ref, cm_ref, rm_ref,
               o_ref, b_ref, f0_ref, f1_ref, f3_ref, m_ref):
    t = pl.program_id(1)
    rows = TR + 2 * RH
    n = rows * wp
    base = pl.multiple_of(t * (TR * wp), 16)
    step = step_ref[...]
    alpha = alpha_ref[...]
    beta = beta_ref[...]
    cm = cm_ref[...]

    xt = x_ref[0, pl.ds(t * TR, rows)].astype(jnp.float32).reshape(n, x_ref.shape[3])
    sb = jnp.dot(xt.astype(jnp.bfloat16), kb_ref[...],
                 preferred_element_type=jnp.float32) * step
    b_ref[...] = sb
    f0 = jnp.maximum(sb, 0.0)
    f0_ref[...] = f0
    inner = (rows - 2) * wp
    f3_ref[pl.ds(2 * wp, inner), :] = f0[wp:(rows - 1) * wp].astype(jnp.bfloat16)

    def update(src_ref, q):
        o = pl.multiple_of(q * wp, 8)
        c = src_ref[pl.ds(o, wp), :]
        up = src_ref[pl.ds(o - wp, wp), :]
        dn = src_ref[pl.ds(o + wp, wp), :]
        lf = pltpu.roll(c, 1, 0)
        rt = pltpu.roll(c, wp - 1, 0)
        nb = (up + dn) + (lf + rt)
        v = (alpha * c + beta * nb) + (b_ref[pl.ds(o, wp), :] - m_ref[pl.ds(o - wp, wp), :])
        return jnp.maximum(v, 0.0)

    m_ref[...] = jnp.dot(f3_ref[pl.ds(2 * wp, inner), :], g3_ref[...],
                         preferred_element_type=jnp.float32)

    def body1(q, carry):
        f1 = update(f0_ref, q) * cm
        f1_ref[pl.ds(pl.multiple_of(q * wp, 8), wp), :] = f1
        return carry

    lax.fori_loop(1, rows - 1, body1, 0, unroll=2)
    for q in (1, rows - 2):
        f1_ref[pl.ds(q * wp, wp), :] = f1_ref[pl.ds(q * wp, wp), :] * rm_ref[t * TR + q]

    f3_ref[pl.ds(2 * wp, inner), :] = f1_ref[pl.ds(wp, inner), :].astype(jnp.bfloat16)
    m_ref[...] = jnp.dot(f3_ref[pl.ds(2 * wp, inner), :], g3_ref[...],
                         preferred_element_type=jnp.float32)

    def body2(q, carry):
        f2 = update(f1_ref, q)
        f2 = pltpu.roll(f2, wp - CH, 0)
        o_ref[0, q - RH] = f2[: wp - 2 * CH]
        return carry

    lax.fori_loop(RH, rows - RH, body2, 0, unroll=2)


def pin(x):
    return with_layout_constraint(x, Layout(tuple(range(x.ndim))))


def per_device(images, rates, smoothing):
    kernel, gram, lam, step = kernel_parts(rates, smoothing)
    kb = kernel.astype(jnp.bfloat16)
    g3 = (gram * step[None, :]).astype(jnp.bfloat16)
    beta = step * lam
    alpha = 1.0 - 4.0 * beta
    x = lax.all_to_all(images, "gy", split_axis=3, concat_axis=0, tiled=True)
    e, sl, h, w = x.shape
    hp, wp = h + 2 * RH, w + 2 * CH
    ny = lax.axis_size("gy")
    dense = Layout((3, 1, 0, 2))
    head = with_layout_constraint(x[..., :CH], dense)
    tail = with_layout_constraint(x[..., w - CH:], dense)
    left = lax.ppermute(tail, "gy", [(i, i + 1) for i in range(ny - 1)])
    right = lax.ppermute(head, "gy", [(i + 1, i) for i in range(ny - 1)])
    x = jnp.concatenate([pin(jnp.transpose(left, (1, 2, 3, 0))),
                         pin(jnp.transpose(x, (1, 2, 3, 0))),
                         pin(jnp.transpose(right, (1, 2, 3, 0)))], axis=2)
    x = pin(x)
    x = pin(halo(x, "gx", 1, RH))
    r = kernel.shape[1]

    gi = lax.axis_index("gx")
    gj = lax.axis_index("gy")
    grow = gi * h + jnp.arange(hp) - RH
    rm = ((grow >= 0) & (grow < h * lax.axis_size("gx"))).astype(jnp.float32)
    gcol = gj * w + jnp.arange(wp) - CH
    cv = ((gcol >= 0) & (gcol < w * lax.axis_size("gy"))).astype(jnp.float32)
    cm = jnp.broadcast_to(cv[:, None], (wp, r))

    rows = TR + 2 * RH
    nt = h // TR
    flops = 2 * sl * nt * rows * wp * r * (e + 2 * r)
    out = pl.pallas_call(
        functools.partial(fit_kernel, wp),
        out_shape=jax.ShapeDtypeStruct((sl, h, w, r), jnp.float32),
        grid=(sl, nt),
        in_specs=[
            pl.BlockSpec((1, hp, wp, e), lambda s, t: (s, 0, 0, 0)),
            pl.BlockSpec((e, r), lambda s, t: (0, 0)),
            pl.BlockSpec((r, r), lambda s, t: (0, 0)),
            pl.BlockSpec((1, r), lambda s, t: (0, 0)),
            pl.BlockSpec((1, r), lambda s, t: (0, 0)),
            pl.BlockSpec((1, r), lambda s, t: (0, 0)),
            pl.BlockSpec((wp, r), lambda s, t: (0, 0)),
            pl.BlockSpec(memory_space=pltpu.SMEM),
        ],
        out_specs=pl.BlockSpec((1, TR, w, r), lambda s, t: (s, t, 0, 0)),
        scratch_shapes=[
            pltpu.VMEM((rows * wp, r), jnp.float32),
            pltpu.VMEM((rows * wp, r), jnp.float32),
            pltpu.VMEM((rows * wp, r), jnp.float32),
            pltpu.VMEM((rows * wp, r), jnp.bfloat16),
            pltpu.VMEM(((rows - 2) * wp, r), jnp.float32),
        ],
        compiler_params=pltpu.CompilerParams(
            dimension_semantics=("arbitrary", "arbitrary"),
            vmem_limit_bytes=48 * 1024 * 1024,
        ),
        cost_estimate=pl.CostEstimate(
            flops=flops, transcendentals=0,
            bytes_accessed=sl * (hp * wp * e * 2 + h * w * r * 4),
        ),
    )(x, kb, g3, step[None, :], alpha[None, :], beta[None, :], cm, rm)
    return out


def solution(mesh):
    in_specs = (P("gy", None, "gx", None), P(), P())
    out_specs = P(None, "gx", "gy", None)
    return jax.shard_map(
        per_device, mesh=mesh, in_specs=in_specs, out_specs=out_specs, check_vma=False
    )
```

```python
import functools

import jax
import jax.numpy as jnp
from jax import lax
from jax.experimental import pallas as pl
from jax.experimental.pallas import tpu as pltpu
from jax.experimental.layout import Layout, with_layout_constraint
from jax.sharding import PartitionSpec as P

E = 64
ITERS = 3
RH = 2
CH = 4
TR = 64


def kernel_parts(rates, smoothing):
    times = 10.0 * (jnp.arange(E, dtype=jnp.float32) + 1.0)
    raw = jnp.exp(-times[:, None] * rates[None, :])
    kernel = raw / jnp.sqrt(jnp.sum(raw * raw, axis=0))[None, :]
    gram = jnp.dot(kernel.T, kernel, precision=lax.Precision.HIGHEST)
    rowsum = jnp.sum(gram, axis=1)
    lam = smoothing * rowsum
    step = 1.0 / (rowsum + 8.0 * lam)
    return (kernel, gram, lam, step)


def halo(cells, axis, dim, width):
    count = lax.axis_size(axis)
    head = lax.slice_in_dim(cells, 0, width, axis=dim)
    tail = lax.slice_in_dim(cells, cells.shape[dim] - width, cells.shape[dim], axis=dim)
    return jnp.concatenate(
        [
            lax.ppermute(tail, axis, [(i, i + 1) for i in range(count - 1)]),
            cells,
            lax.ppermute(head, axis, [(i + 1, i) for i in range(count - 1)]),
        ],
        axis=dim,
    )


def fit_kernel(wp, x_ref, kb_ref, g3_ref, step_ref, alpha_ref, beta_ref, cm_ref, rm_ref,
               o_ref, b_ref, f0_ref, f1_ref, f3_ref, m_ref):
    t = pl.program_id(1)
    rows = TR + 2 * RH
    n = rows * wp
    base = pl.multiple_of(t * (TR * wp), 16)
    step = step_ref[...]
    alpha = alpha_ref[...]
    beta = beta_ref[...]
    cm = cm_ref[...]

    xt = x_ref[0, pl.ds(t * TR, rows)].astype(jnp.float32).reshape(n, x_ref.shape[3])
    b_ref[...] = jnp.dot(xt.astype(jnp.bfloat16), kb_ref[...],
                         preferred_element_type=jnp.float32)
    inner = (rows - 2) * wp
    for q in (0, rows - 1):
        sb = b_ref[pl.ds(q * wp, wp), :] * step
        b_ref[pl.ds(q * wp, wp), :] = sb
        f0_ref[pl.ds(q * wp, wp), :] = jnp.maximum(sb, 0.0)

    def body0(k, carry):
        o = pl.multiple_of((2 * k + 1) * wp, 8)
        sb = b_ref[pl.ds(o, 2 * wp), :] * step
        b_ref[pl.ds(o, 2 * wp), :] = sb
        f0 = jnp.maximum(sb, 0.0)
        f0_ref[pl.ds(o, 2 * wp), :] = f0
        f3_ref[pl.ds(pl.multiple_of(o + wp, 16), 2 * wp), :] = f0.astype(jnp.bfloat16)
        return carry

    lax.fori_loop(0, (rows - 2) // 2, body0, 0)

    def update(src_ref, q):
        o = pl.multiple_of(q * wp, 8)
        c = src_ref[pl.ds(o, wp), :]
        up = src_ref[pl.ds(o - wp, wp), :]
        dn = src_ref[pl.ds(o + wp, wp), :]
        lf = pltpu.roll(c, 1, 0)
        rt = pltpu.roll(c, wp - 1, 0)
        nb = (up + dn) + (lf + rt)
        v = (alpha * c + beta * nb) + (b_ref[pl.ds(o, wp), :] - m_ref[pl.ds(o - wp, wp), :])
        return jnp.maximum(v, 0.0)

    m_ref[...] = jnp.dot(f3_ref[pl.ds(2 * wp, inner), :], g3_ref[...],
                         preferred_element_type=jnp.float32)

    def body1(q, carry):
        f1 = update(f0_ref, q) * cm
        f1_ref[pl.ds(pl.multiple_of(q * wp, 8), wp), :] = f1
        return carry

    lax.fori_loop(1, rows - 1, body1, 0, unroll=2)
    for q in (1, rows - 2):
        f1_ref[pl.ds(q * wp, wp), :] = f1_ref[pl.ds(q * wp, wp), :] * rm_ref[t * TR + q]

    f3_ref[pl.ds(2 * wp, inner), :] = f1_ref[pl.ds(wp, inner), :].astype(jnp.bfloat16)
    m_ref[...] = jnp.dot(f3_ref[pl.ds(2 * wp, inner), :], g3_ref[...],
                         preferred_element_type=jnp.float32)

    def body2(q, carry):
        f2 = update(f1_ref, q)
        f2 = pltpu.roll(f2, wp - CH, 0)
        o_ref[0, q - RH] = f2[: wp - 2 * CH]
        return carry

    lax.fori_loop(RH, rows - RH, body2, 0, unroll=2)


def pin(x):
    return with_layout_constraint(x, Layout(tuple(range(x.ndim))))


def per_device(images, rates, smoothing):
    kernel, gram, lam, step = kernel_parts(rates, smoothing)
    kb = kernel.astype(jnp.bfloat16)
    g3 = (gram * step[None, :]).astype(jnp.bfloat16)
    beta = step * lam
    alpha = 1.0 - 4.0 * beta
    x = lax.all_to_all(images, "gy", split_axis=3, concat_axis=0, tiled=True)
    e, sl, h, w = x.shape
    hp, wp = h + 2 * RH, w + 2 * CH
    ny = lax.axis_size("gy")
    dense = Layout((3, 1, 0, 2))
    head = with_layout_constraint(x[..., :CH], dense)
    tail = with_layout_constraint(x[..., w - CH:], dense)
    left = lax.ppermute(tail, "gy", [(i, i + 1) for i in range(ny - 1)])
    right = lax.ppermute(head, "gy", [(i + 1, i) for i in range(ny - 1)])
    x = jnp.concatenate([pin(jnp.transpose(left, (1, 2, 3, 0))),
                         pin(jnp.transpose(x, (1, 2, 3, 0))),
                         pin(jnp.transpose(right, (1, 2, 3, 0)))], axis=2)
    x = pin(x)
    x = pin(halo(x, "gx", 1, RH))
    r = kernel.shape[1]

    gi = lax.axis_index("gx")
    gj = lax.axis_index("gy")
    grow = gi * h + jnp.arange(hp) - RH
    rm = ((grow >= 0) & (grow < h * lax.axis_size("gx"))).astype(jnp.float32)
    gcol = gj * w + jnp.arange(wp) - CH
    cv = ((gcol >= 0) & (gcol < w * lax.axis_size("gy"))).astype(jnp.float32)
    cm = jnp.broadcast_to(cv[:, None], (wp, r))

    rows = TR + 2 * RH
    nt = h // TR
    flops = 2 * sl * nt * rows * wp * r * (e + 2 * r)
    out = pl.pallas_call(
        functools.partial(fit_kernel, wp),
        out_shape=jax.ShapeDtypeStruct((sl, h, w, r), jnp.float32),
        grid=(sl, nt),
        in_specs=[
            pl.BlockSpec((1, hp, wp, e), lambda s, t: (s, 0, 0, 0)),
            pl.BlockSpec((e, r), lambda s, t: (0, 0)),
            pl.BlockSpec((r, r), lambda s, t: (0, 0)),
            pl.BlockSpec((1, r), lambda s, t: (0, 0)),
            pl.BlockSpec((1, r), lambda s, t: (0, 0)),
            pl.BlockSpec((1, r), lambda s, t: (0, 0)),
            pl.BlockSpec((wp, r), lambda s, t: (0, 0)),
            pl.BlockSpec(memory_space=pltpu.SMEM),
        ],
        out_specs=pl.BlockSpec((1, TR, w, r), lambda s, t: (s, t, 0, 0)),
        scratch_shapes=[
            pltpu.VMEM((rows * wp, r), jnp.float32),
            pltpu.VMEM((rows * wp, r), jnp.float32),
            pltpu.VMEM((rows * wp, r), jnp.float32),
            pltpu.VMEM((rows * wp, r), jnp.bfloat16),
            pltpu.VMEM(((rows - 2) * wp, r), jnp.float32),
        ],
        compiler_params=pltpu.CompilerParams(
            dimension_semantics=("arbitrary", "arbitrary"),
            vmem_limit_bytes=48 * 1024 * 1024,
        ),
        cost_estimate=pl.CostEstimate(
            flops=flops, transcendentals=0,
            bytes_accessed=sl * (hp * wp * e * 2 + h * w * r * 4),
        ),
    )(x, kb, g3, step[None, :], alpha[None, :], beta[None, :], cm, rm)
    return out


def solution(mesh):
    in_specs = (P("gy", None, "gx", None), P(), P())
    out_specs = P(None, "gx", "gy", None)
    return jax.shard_map(
        per_device, mesh=mesh, in_specs=in_specs, out_specs=out_specs, check_vma=False
    )
```

```python
import functools

import jax
import jax.numpy as jnp
from jax import lax
from jax.experimental import pallas as pl
from jax.experimental.pallas import tpu as pltpu
from jax.experimental.layout import Layout, with_layout_constraint
from jax.sharding import PartitionSpec as P

E = 64
ITERS = 3
RH = 2
CH = 4
TR = 64


def kernel_parts(rates, smoothing):
    times = 10.0 * (jnp.arange(E, dtype=jnp.float32) + 1.0)
    raw = jnp.exp(-times[:, None] * rates[None, :])
    kernel = raw / jnp.sqrt(jnp.sum(raw * raw, axis=0))[None, :]
    gram = jnp.dot(kernel.T, kernel, precision=lax.Precision.HIGHEST)
    rowsum = jnp.sum(gram, axis=1)
    lam = smoothing * rowsum
    step = 1.0 / (rowsum + 8.0 * lam)
    return (kernel, gram, lam, step)


def halo(cells, axis, dim, width):
    count = lax.axis_size(axis)
    head = lax.slice_in_dim(cells, 0, width, axis=dim)
    tail = lax.slice_in_dim(cells, cells.shape[dim] - width, cells.shape[dim], axis=dim)
    return jnp.concatenate(
        [
            lax.ppermute(tail, axis, [(i, i + 1) for i in range(count - 1)]),
            cells,
            lax.ppermute(head, axis, [(i + 1, i) for i in range(count - 1)]),
        ],
        axis=dim,
    )


def fit_kernel(wp, x_ref, kb_ref, g3_ref, step_ref, alpha_ref, beta_ref, cm_ref, rm_ref,
               o_ref, b_ref, f0_ref, f1_ref, f3_ref, m_ref):
    t = pl.program_id(1)
    rows = TR + 2 * RH
    n = rows * wp
    base = pl.multiple_of(t * (TR * wp), 16)
    step = step_ref[...]
    alpha = alpha_ref[...]
    beta = beta_ref[...]
    cm = cm_ref[...]

    xt = x_ref[0, pl.ds(t * TR, rows)].astype(jnp.float32).reshape(n, x_ref.shape[3])
    sb = jnp.dot(xt.astype(jnp.bfloat16), kb_ref[...],
                 preferred_element_type=jnp.float32) * step
    b_ref[...] = sb
    f0 = jnp.maximum(sb, 0.0)
    f0_ref[...] = f0
    inner = (rows - 2) * wp
    f3_ref[pl.ds(2 * wp, inner), :] = f0[wp:(rows - 1) * wp].astype(jnp.bfloat16)

    def update(src_ref, q):
        o = pl.multiple_of(q * wp, 8)
        c = src_ref[pl.ds(o, wp), :]
        up = src_ref[pl.ds(o - wp, wp), :]
        dn = src_ref[pl.ds(o + wp, wp), :]
        lf = pltpu.roll(c, 1, 0)
        rt = pltpu.roll(c, wp - 1, 0)
        nb = (up + dn) + (lf + rt)
        v = (alpha * c + beta * nb) + (b_ref[pl.ds(o, wp), :] - m_ref[pl.ds(o - wp, wp), :])
        return jnp.maximum(v, 0.0)

    m_ref[...] = jnp.dot(f3_ref[pl.ds(2 * wp, inner), :], g3_ref[...],
                         preferred_element_type=jnp.float32)

    def body1(q, carry):
        f1 = update(f0_ref, q) * cm
        f1_ref[pl.ds(pl.multiple_of(q * wp, 8), wp), :] = f1
        return carry

    lax.fori_loop(1, rows - 1, body1, 0)
    for q in (1, rows - 2):
        f1_ref[pl.ds(q * wp, wp), :] = f1_ref[pl.ds(q * wp, wp), :] * rm_ref[t * TR + q]

    f3_ref[pl.ds(2 * wp, inner), :] = f1_ref[pl.ds(wp, inner), :].astype(jnp.bfloat16)
    m_ref[...] = jnp.dot(f3_ref[pl.ds(2 * wp, inner), :], g3_ref[...],
                         preferred_element_type=jnp.float32)

    def body2(q, carry):
        f2 = update(f1_ref, q)
        f2 = pltpu.roll(f2, wp - CH, 0)
        o_ref[0, q - RH] = f2[: wp - 2 * CH]
        return carry

    lax.fori_loop(RH, rows - RH, body2, 0, unroll=2)


def pin(x):
    return with_layout_constraint(x, Layout(tuple(range(x.ndim))))


def per_device(images, rates, smoothing):
    kernel, gram, lam, step = kernel_parts(rates, smoothing)
    kb = kernel.astype(jnp.bfloat16)
    g3 = (gram * step[None, :]).astype(jnp.bfloat16)
    beta = step * lam
    alpha = 1.0 - 4.0 * beta
    x = lax.all_to_all(images, "gy", split_axis=3, concat_axis=0, tiled=True)
    e, sl, h, w = x.shape
    hp, wp = h + 2 * RH, w + 2 * CH
    ny = lax.axis_size("gy")
    dense = Layout((3, 1, 0, 2))
    head = with_layout_constraint(x[..., :CH], dense)
    tail = with_layout_constraint(x[..., w - CH:], dense)
    left = lax.ppermute(tail, "gy", [(i, i + 1) for i in range(ny - 1)])
    right = lax.ppermute(head, "gy", [(i + 1, i) for i in range(ny - 1)])
    x = jnp.concatenate([pin(jnp.transpose(left, (1, 2, 3, 0))),
                         pin(jnp.transpose(x, (1, 2, 3, 0))),
                         pin(jnp.transpose(right, (1, 2, 3, 0)))], axis=2)
    x = pin(x)
    x = pin(halo(x, "gx", 1, RH))
    r = kernel.shape[1]

    gi = lax.axis_index("gx")
    gj = lax.axis_index("gy")
    grow = gi * h + jnp.arange(hp) - RH
    rm = ((grow >= 0) & (grow < h * lax.axis_size("gx"))).astype(jnp.float32)
    gcol = gj * w + jnp.arange(wp) - CH
    cv = ((gcol >= 0) & (gcol < w * lax.axis_size("gy"))).astype(jnp.float32)
    cm = jnp.broadcast_to(cv[:, None], (wp, r))

    rows = TR + 2 * RH
    nt = h // TR
    flops = 2 * sl * nt * rows * wp * r * (e + 2 * r)
    out = pl.pallas_call(
        functools.partial(fit_kernel, wp),
        out_shape=jax.ShapeDtypeStruct((sl, h, w, r), jnp.float32),
        grid=(sl, nt),
        in_specs=[
            pl.BlockSpec((1, hp, wp, e), lambda s, t: (s, 0, 0, 0)),
            pl.BlockSpec((e, r), lambda s, t: (0, 0)),
            pl.BlockSpec((r, r), lambda s, t: (0, 0)),
            pl.BlockSpec((1, r), lambda s, t: (0, 0)),
            pl.BlockSpec((1, r), lambda s, t: (0, 0)),
            pl.BlockSpec((1, r), lambda s, t: (0, 0)),
            pl.BlockSpec((wp, r), lambda s, t: (0, 0)),
            pl.BlockSpec(memory_space=pltpu.SMEM),
        ],
        out_specs=pl.BlockSpec((1, TR, w, r), lambda s, t: (s, t, 0, 0)),
        scratch_shapes=[
            pltpu.VMEM((rows * wp, r), jnp.float32),
            pltpu.VMEM((rows * wp, r), jnp.float32),
            pltpu.VMEM((rows * wp, r), jnp.float32),
            pltpu.VMEM((rows * wp, r), jnp.bfloat16),
            pltpu.VMEM(((rows - 2) * wp, r), jnp.float32),
        ],
        compiler_params=pltpu.CompilerParams(
            dimension_semantics=("arbitrary", "arbitrary"),
            vmem_limit_bytes=48 * 1024 * 1024,
        ),
        cost_estimate=pl.CostEstimate(
            flops=flops, transcendentals=0,
            bytes_accessed=sl * (hp * wp * e * 2 + h * w * r * 4),
        ),
    )(x, kb, g3, step[None, :], alpha[None, :], beta[None, :], cm, rm)
    return out


def solution(mesh):
    in_specs = (P("gy", None, "gx", None), P(), P())
    out_specs = P(None, "gx", "gy", None)
    return jax.shard_map(
        per_device, mesh=mesh, in_specs=in_specs, out_specs=out_specs, check_vma=False
    )
```
